32 devices in a mesh: groups: 2 (over x), ctx: 16 (over z, y, core).
Axes of the slice: x: 2, y: 2, z: 4, core: 2. Of those that a mesh axis runs over, the one named last changes fastest.
Arguments:
- queries: bfloat16 [8192, 2048], P(('groups', 'ctx')), parts along dimension 0, may hold values from -14 to 14
- keys: bfloat16 [8192, 512], P(('groups', 'ctx')), parts along dimension 0, may hold values from -6 to 6
- values: bfloat16 [8192, 512], P(('groups', 'ctx')), parts along dimension 0, may hold values from -6 to 6
- doc_starts: int32 [32, 2], P(('groups', 'ctx')), parts along dimension 0, may hold values from -1 to 31, as said below
Outputs:
- attended: bfloat16 [8192, 2048], P(('groups', 'ctx')), parts along dimension 0
The draws below stay inside these ranges and needn't reach their ends.
There are 2 independent parts, one for each index of `groups`. The reference program is written for one: setup_inputs(seed, part) draws one part's arguments, and reference() takes and returns one part's arrays. A program takes and returns all parts, laid end to end along the dimension named above; each array names one. Nothing has to cross between parts.
Inputs may be any that keep to these rules, and one draw needn't show every extreme that they name: `doc_starts`: row c lists, rising, the global indices of the blocks of 128 tokens in tokens c * 256 .. (c + 1) * 256 - 1 at which a document begins, then -1 in the remaining slots. The first document begins in row 0 after block 0; no document begins in row 1; a document begins at the last block.
All inputs are finite; a program needn't handle non-finite values.
Results may differ from the reference program's by a relative error of at most 0.0032.
Values may be sent and summed in bfloat16 or wider, within the bound.
No kernel may reach another device: no remote copies, remote signals or barrier semaphores. Data moves between devices by JAX's collectives and lax.ppermute only.
A program may use at most 64 MiB of HBM per device.

```python
import math
import jax
import jax.numpy as jnp
from jax import lax

H = 16
KV = 4
HD = 128
WINDOW = 2048
BLK = 128
TOK_DEV = 256
TOKENS = 4096
REACH = 8
N_CTX = 16


def paired_fields(key):
    query_key = jax.random.fold_in(key, 11)
    key_key = jax.random.fold_in(key, 12)
    query_shape = (TOKENS, H * HD)
    key_shape = (TOKENS, KV * HD)
    queries = jnp.clip(jax.random.normal(query_key, query_shape, jnp.float32) * 2.2, -13.0, 13.0)
    keyset = jnp.clip(jax.random.normal(key_key, key_shape, jnp.float32), -6.0, 6.0)
    return (queries, keyset)


def draw_queries(key, part):
    return paired_fields(key)[0].astype(jnp.bfloat16)


def draw_keys(key, part):
    return paired_fields(key)[1].astype(jnp.bfloat16)


def draw_doc_starts(key, part):
    block_total = TOKENS // BLK
    per_stretch = TOK_DEV // BLK
    blocks = jnp.arange(block_total, dtype=jnp.int32)
    coins = jax.random.randint(jax.random.fold_in(key, 21), (block_total,), 0, 6) == 0
    first_start = jax.random.randint(jax.random.fold_in(key, 22), (), 1, per_stretch)
    flags = jnp.where(blocks < 2 * per_stretch, blocks == first_start, coins | (blocks == block_total - 1))
    flags = flags.reshape(-1, per_stretch)
    within = jnp.arange(per_stretch, dtype=jnp.int32)
    ranking = jnp.where(flags, within[None, :], per_stretch + within[None, :])
    ordering = jnp.argsort(ranking, axis=1, stable=True)
    listed = jnp.where(flags, blocks.reshape(-1, per_stretch), -1)
    return jnp.take_along_axis(listed, ordering, axis=1).astype(jnp.int32)


def block_scale(stream_key, shape, cuts, least, largest):
    gain, own = 1.0, jax.random.fold_in(stream_key, 6)
    for position, blocks in cuts:
        heights = jnp.exp(jax.random.uniform(jax.random.fold_in(own, position), (blocks,), jnp.float32, least / len(cuts), largest / len(cuts)))
        gain = gain * jnp.repeat(heights, shape[position] // blocks).reshape([-1 if axis == position else 1 for axis in range(len(shape))])
    return gain


def bell_draw(key, shape, scale, reach, split=(), kind=jnp.bfloat16):
    array = jax.random.normal(key, shape, jnp.float32) * scale
    if len(split) > 0:
        array = block_scale(key, shape, split, -0.22, 0.18) * array
    return jnp.clip(array, min=-reach, max=reach).astype(kind)


def setup_inputs(seed: int = 0, part: int = 0) -> dict:
    seeds = jax.random.split(jax.random.key(seed), 5)
    part_splits = jax.random.split(jax.random.fold_in(seeds[4], part), 5)
    return {
        "queries": draw_queries(jax.random.fold_in(jax.random.fold_in(seeds[4], part), 71), part),
        "keys": draw_keys(jax.random.fold_in(jax.random.fold_in(seeds[4], part), 71), part),
        "values": bell_draw(part_splits[2], (TOKENS, KV * HD), 1.0, 6.0, ((0, 16),)),
        "doc_starts": draw_doc_starts(jax.random.fold_in(jax.random.fold_in(seeds[4], part), 71), part),
    }


masked_value = -1e+30

def block_starts(doc_starts):
    flat = doc_starts.reshape(-1)
    blocks = jnp.arange(TOKENS // BLK, dtype=jnp.int32)
    return lax.optimization_barrier(jnp.max(jnp.where(flat[None, :] <= blocks[:, None], flat[None, :], -1), axis=1))

def attend_stretch(query_rows, key_rows, value_rows, start_tok, first_pos):
    length = query_rows.shape[0]
    key_span = key_rows.shape[0]
    query_pos = first_pos + jnp.arange(length, dtype=jnp.int32)
    key_pos = first_pos - (key_span - length) + jnp.arange(key_span, dtype=jnp.int32)
    visible = (key_pos[None, :] <= query_pos[:, None]) & (query_pos[:, None] - key_pos[None, :] < WINDOW)
    visible = visible & (jnp.floor_divide(key_pos, BLK)[None, :] >= start_tok[:, None])
    active = start_tok >= 0
    per_group = H // KV
    scaling = 1.0 / math.sqrt(HD)

    def head_fn(head_index):
        kv_group = head_index // per_group
        q_head = lax.dynamic_slice_in_dim(query_rows, head_index * HD, HD, 1)
        k_head = lax.dynamic_slice_in_dim(key_rows, kv_group * HD, HD, 1)
        v_head = lax.dynamic_slice_in_dim(value_rows, kv_group * HD, HD, 1)
        scores = jnp.dot(q_head, k_head.T, preferred_element_type=jnp.float32) * scaling
        scores = jnp.where(visible, scores, masked_value)
        row_peak = lax.optimization_barrier(jnp.max(scores, axis=1, keepdims=True))
        weights = jnp.exp(scores - row_peak)
        row_total = lax.optimization_barrier(jnp.sum(weights, axis=1, keepdims=True))
        blended = jnp.dot(weights.astype(jnp.bfloat16), v_head, preferred_element_type=jnp.float32) / row_total
        return jnp.where(active[:, None], blended, 0.0).astype(jnp.bfloat16)
    stacked = lax.map(head_fn, jnp.arange(H, dtype=jnp.int32))
    return jnp.transpose(stacked, (1, 0, 2)).reshape(length, H * HD)

def reference(queries, keys, values, doc_starts):
    start_tok = jnp.repeat(block_starts(doc_starts), BLK)
    front = jnp.zeros((REACH * TOK_DEV, KV * HD), keys.dtype)
    keys_padded = jnp.concatenate([front, keys], 0)
    values_padded = jnp.concatenate([front, values], 0)

    def stretch_fn(stretch):
        first = (stretch * TOK_DEV).astype(jnp.int32)
        return attend_stretch(lax.dynamic_slice_in_dim(queries, first, TOK_DEV, 0), lax.dynamic_slice_in_dim(keys_padded, first, (REACH + 1) * TOK_DEV, 0), lax.dynamic_slice_in_dim(values_padded, first, (REACH + 1) * TOK_DEV, 0), lax.dynamic_slice_in_dim(start_tok, first, TOK_DEV, 0), first)
    stacked = lax.map(stretch_fn, jnp.arange(N_CTX, dtype=jnp.int32))
    return stacked.reshape(TOKENS, H * HD)
```

```python
import functools
import math

import jax
import jax.numpy as jnp
from jax import lax
from jax.experimental import pallas as pl
from jax.experimental.pallas import tpu as pltpu
from jax.sharding import PartitionSpec as P

HD = 128
WINDOW = 2048
BLK = 128
LEN = 256
GROUP = 4
MASKED = -1e30
COEF = math.log2(math.e) / math.sqrt(HD)

VMEM = pl.BlockSpec(memory_space=pltpu.VMEM)
SMEM = pl.BlockSpec(memory_space=pltpu.SMEM)


def exchanged(x, bit):
    n = lax.axis_size("ctx")
    return lax.ppermute(x, "ctx", [(i, i ^ bit) for i in range(n)])


def shifted(x, distance):
    n = lax.axis_size("ctx")
    return lax.ppermute(x, "ctx", [(i, (i + distance) % n) for i in range(n)])


def half(core):
    return pl.ds(pl.multiple_of(core * 256, 256), 256)


def prep_kv_kernel(k_ref, v_ref, keep_ref, send_ref):
    core = lax.rem(lax.axis_index("ctx"), 2)
    for ref, pick in ((keep_ref, core), (send_ref, 1 - core)):
        ref[:, :256] = k_ref[:, half(pick)]
        ref[:, 256:] = v_ref[:, half(pick)]


def prep_q_kernel(q_ref, keep_ref, send_ref):
    core = lax.rem(lax.axis_index("ctx"), 2)
    width = keep_ref.shape[1]
    for ref, pick in ((keep_ref, core), (send_ref, 1 - core)):
        ref[...] = q_ref[:, pl.ds(pl.multiple_of(pick * width, width), width)]


def merge_kernel(keep_ref, got_ref, out_ref):
    core = lax.rem(lax.axis_index("ctx"), 2)
    width = keep_ref.shape[1]
    for ref, pick in ((keep_ref, core), (got_ref, 1 - core)):
        out_ref[:, pl.ds(pl.multiple_of(pick * width, width), width)] = ref[...]


def block_start(tables, block):
    best = jnp.int32(-1)
    for table in tables:
        for row in range(table.shape[0]):
            for col in range(table.shape[1]):
                entry = table[row, col]
                best = jnp.maximum(best, jnp.where(entry <= block, entry, -1))
    return best


def head_step(q_ref, acc_ref, ml_ref, tile, head, k_tile, v_turned, bounds):
    heads = acc_ref.shape[1]
    q_head = q_ref[tile, :, pl.ds(pl.multiple_of(head * HD, HD), HD)]
    scores = lax.dot_general(
        k_tile, q_head, (((1,), (1,)), ((), ())), preferred_element_type=jnp.float32
    )
    if bounds is not None:
        scores = jnp.where(bounds, scores, MASKED)
    old = ml_ref[tile, head]
    new = jnp.maximum(old, jnp.max(scores, axis=0, keepdims=True))
    weights = jnp.exp2((scores - new) * COEF)
    fade = jnp.exp2((old - new) * COEF)
    ml_ref[tile, head] = new
    ml_ref[tile, heads + head] = ml_ref[tile, heads + head] * fade + jnp.sum(
        weights, axis=0, keepdims=True
    )
    product = jnp.dot(v_turned, weights.astype(jnp.bfloat16), preferred_element_type=jnp.float32)
    acc_ref[tile, head] = acc_ref[tile, head] * fade + product


def attend_kernel(sources, n_tables, first, last, *refs):
    refs = list(refs)
    take = lambda n: [refs.pop(0) for _ in range(n)]
    tables = take(n_tables)
    q_in = take(2)
    chunk_in = take(len(sources))
    state_in = [] if first else take(2)
    outs = take(2)
    q_ref, chunk_ref, acc_ref, ml_ref, q_sem, chunk_sem, state_sem = refs
    count = len(sources)
    stretch = lax.axis_index("ctx")
    heads = acc_ref.shape[1]

    low = [block_start(tables, 2 * (stretch ^ tile)) for tile in range(2)]
    high = [block_start(tables, 2 * (stretch ^ tile) + 1) for tile in range(2)]
    source_of = [(stretch ^ bits) - back for bits, back in sources]

    def limit(tile):
        return jnp.maximum(low[tile] * BLK, (stretch ^ tile) * LEN - WINDOW + 1)

    def seen(source, tile):
        return (source >= 0) & (source <= (stretch ^ tile)) & (source * LEN + LEN > limit(tile))

    used = [seen(source, 0) | seen(source, 1) for source in source_of]
    busy = functools.reduce(jnp.logical_or, used)

    q_copies = [pltpu.make_async_copy(q_in[i], q_ref.at[i], q_sem.at[i]) for i in range(2)]
    chunk_copies = [
        pltpu.make_async_copy(chunk_in[i], chunk_ref.at[i], chunk_sem.at[i]) for i in range(count)
    ]
    state_copies = [
        pltpu.make_async_copy(source, target, state_sem.at[i])
        for i, (source, target) in enumerate(zip(state_in, (acc_ref, ml_ref)))
    ]

    def work():
        for copy in q_copies:
            copy.start()
        for copy, wanted in zip(chunk_copies, used):
            pl.when(wanted)(copy.start)
        if first:
            acc_ref[...] = jnp.zeros_like(acc_ref)
            ml_ref[:, :heads] = jnp.full_like(ml_ref[:, :heads], MASKED)
            ml_ref[:, heads:] = jnp.zeros_like(ml_ref[:, heads:])
        elif not last:
            for copy in state_copies:
                copy.start()
        for copy in q_copies:
            copy.wait()
        if not first:
            for copy in state_copies:
                copy.wait()
        for copy, wanted in zip(chunk_copies, used):
            pl.when(wanted)(copy.wait)

        def visit(step, _):
            chunk, tile = lax.div(step, 2), lax.rem(step, 2)
            where = stretch ^ tile
            source = source_of[0]
            for i in range(1, count):
                source = jnp.where(chunk == i, source_of[i], source)
            low_start = jnp.where(tile == 0, low[0], low[1])
            high_start = jnp.where(tile == 0, high[0], high[1])
            first_key, first_query = source * LEN, where * LEN
            low_limit = jnp.maximum(low_start * BLK, first_query - WINDOW + 1)
            in_view = (source >= 0) & (source <= where) & (first_key + LEN > low_limit)
            high_limit = jnp.maximum(high_start * BLK, first_query + LEN - WINDOW)
            whole = (source < where) & (first_key >= high_limit)

            def all_heads(masked):
                bounds = None
                if masked:
                    lane = lax.broadcasted_iota(jnp.int32, (1, LEN), 1)
                    query_pos = first_query + lane
                    start = jnp.where(lane < BLK, low_start, high_start) * BLK
                    least = jnp.maximum(start, query_pos - (WINDOW - 1))
                    key_pos = first_key + lax.broadcasted_iota(jnp.int32, (LEN, LEN), 0)
                    bounds = (key_pos <= query_pos) & (key_pos >= least)

                def one_pair(pair, _):
                    k_tile = chunk_ref[chunk, :, pl.ds(pl.multiple_of(pair * HD, HD), HD)]
                    v_tile = chunk_ref[chunk, :, pl.ds(pl.multiple_of((2 + pair) * HD, HD), HD)]
                    v_turned = v_tile.T
                    for sub in range(GROUP):
                        head_step(
                            q_ref, acc_ref, ml_ref, tile, pair * GROUP + sub, k_tile, v_turned, bounds
                        )
                    return 0

                lax.fori_loop(0, heads // GROUP, one_pair, 0)

            @pl.when(in_view & whole)
            def _():
                all_heads(False)

            @pl.when(in_view & jnp.logical_not(whole))
            def _():
                all_heads(True)

            return 0

        lax.fori_loop(0, 2 * count, visit, 0)
        if not last:
            back = [
                pltpu.make_async_copy(source, target, state_sem.at[i])
                for i, (source, target) in enumerate(zip((acc_ref, ml_ref), outs))
            ]
            for copy in back:
                copy.start()
            for copy in back:
                copy.wait()

    if first:
        work()
    elif not last:
        pl.when(busy)(work)
    else:
        for copy in state_copies:
            copy.start()
        pl.when(busy)(work)

        @pl.when(jnp.logical_not(busy))
        def _():
            for copy in state_copies:
                copy.wait()

        earlier = stretch >= 12
        for tile, out_ref in enumerate(outs):
            lane = lax.broadcasted_iota(jnp.int32, (1, LEN), 1)
            start = jnp.where(lane < BLK, low[tile], high[tile])
            active = (start >= 0) | earlier

            def finish(head, _, tile=tile, out_ref=out_ref, active=active):
                scale = jnp.where(active, 1.0 / ml_ref[tile, heads + head], 0.0)
                blended = acc_ref[tile, head] * scale
                out_ref[:, pl.ds(pl.multiple_of(head * HD, HD), HD)] = blended.T.astype(jnp.bfloat16)
                return 0

            lax.fori_loop(0, heads, finish, 0)


def attend(tables, qs, chunks, sources, state, last=False):
    heads = qs[0].shape[1] // HD
    first = state is None
    any_space = pl.BlockSpec(memory_space=pl.ANY)
    args = list(tables) + list(qs) + list(chunks)
    specs = [SMEM] * len(tables) + [any_space] * (2 + len(chunks))
    acc_shape, ml_shape = (2, heads, HD, LEN), (2, 2 * heads, 1, LEN)
    aliases = {}
    if not first:
        if not last:
            aliases = {len(args): 0, len(args) + 1: 1}
        args += list(state)
        specs += [any_space] * 2
    if last:
        shapes = [jax.ShapeDtypeStruct(qs[0].shape, jnp.bfloat16)] * 2
    else:
        shapes = [jax.ShapeDtypeStruct(s, jnp.float32) for s in (acc_shape, ml_shape)]
    flops = len(chunks) * 2 * heads * LEN * LEN * HD * 4
    return pl.pallas_call(
        functools.partial(attend_kernel, sources, len(tables), first, last),
        out_shape=shapes,
        in_specs=specs,
        out_specs=[VMEM if last else any_space] * 2,
        scratch_shapes=[
            pltpu.VMEM((2,) + qs[0].shape, jnp.bfloat16),
            pltpu.VMEM((len(chunks),) + chunks[0].shape, jnp.bfloat16),
            pltpu.VMEM(acc_shape, jnp.float32),
            pltpu.VMEM(ml_shape, jnp.float32),
            pltpu.SemaphoreType.DMA((2,)),
            pltpu.SemaphoreType.DMA((len(chunks),)),
            pltpu.SemaphoreType.DMA((2,)),
        ],
        input_output_aliases=aliases,
        cost_estimate=pl.CostEstimate(
            flops=flops, bytes_accessed=4 << 20, transcendentals=len(chunks) * 2 * heads * LEN * LEN
        ),
        name="attend",
    )(*args)


def split_call(kernel, args, shapes, name):
    return pl.pallas_call(
        kernel,
        out_shape=[jax.ShapeDtypeStruct(s, jnp.bfloat16) for s in shapes],
        in_specs=[VMEM] * len(args),
        out_specs=[VMEM] * len(shapes),
        name=name,
    )(*args)


def on_device(queries, keys, values, doc_starts):
    rows, width = queries.shape
    assert rows == LEN and keys.shape[1] == 4 * HD and lax.axis_size("ctx") % 4 == 0
    own, send = split_call(prep_kv_kernel, (keys, values), [(LEN, 512)] * 2, "prep_kv")
    a_own = shifted(own, 4)
    pair = exchanged(send, 1)
    q_keep, q_send = split_call(prep_q_kernel, (queries,), [(LEN, width // 2)] * 2, "prep_q")
    q_pair = exchanged(q_send, 1)
    quad = jnp.concatenate([doc_starts] + [exchanged(doc_starts, bit) for bit in (1, 2, 3)], 0)
    a_pair = shifted(pair, 4)
    y_own = exchanged(own, 2)
    y_pair = exchanged(pair, 2)
    quad_1 = shifted(quad, 4)
    quad_2 = shifted(quad_1, 4)
    b_own = shifted(a_own, 4)
    b_pair = shifted(a_pair, 4)
    ya_own = exchanged(a_own, 2)
    ya_pair = exchanged(a_pair, 2)
    yb_own = exchanged(b_own, 2)
    yb_pair = exchanged(b_pair, 2)
    qs = (q_keep, q_pair)
    tables = (quad, quad_1, quad_2)
    state = attend(tables[:1], qs, (own, pair), ((0, 0), (1, 0)), None)
    state = attend(
        tables[:2], qs, (y_own, y_pair, a_own, a_pair), ((2, 0), (3, 0), (0, 4), (1, 4)), state
    )
    state = attend(tables[:2], qs, (ya_own, ya_pair), ((2, 4), (3, 4)), state)
    state = attend(tables, qs, (b_own, b_pair, yb_own), ((0, 8), (1, 8), (2, 8)), state)
    out_keep, out_send = attend(tables, qs, (yb_pair,), ((3, 8),), state, last=True)
    out_got = exchanged(out_send, 1)
    return split_call(merge_kernel, (out_keep, out_got), [(LEN, width)], "merge")[0]


def solution(mesh):
    spec = P(("groups", "ctx"), None)
    return jax.shard_map(
        on_device, mesh=mesh, in_specs=(spec,) * 4, out_specs=spec, check_vma=False
    )
```

```python
import functools
import math

import jax
import jax.numpy as jnp
from jax import lax
from jax.experimental import pallas as pl
from jax.experimental.pallas import tpu as pltpu
from jax.sharding import PartitionSpec as P

HD = 128
WINDOW = 2048
BLK = 128
LEN = 256
GROUP = 4
WIDE = GROUP * LEN
INFO = 2 * LEN
CHUNK = (INFO + 16, LEN)
MASKED = -1e30
COEF = math.log2(math.e) / math.sqrt(HD)

VMEM = pl.BlockSpec(memory_space=pltpu.VMEM)
SMEM = pl.BlockSpec(memory_space=pltpu.SMEM)
ANY = pl.BlockSpec(memory_space=pl.ANY)
LIMIT = 20 << 20


def exchanged(x, bit):
    n = lax.axis_size("ctx")
    return lax.ppermute(x, "ctx", [(i, i ^ bit) for i in range(n)])


def shifted(x, distance):
    n = lax.axis_size("ctx")
    return lax.ppermute(x, "ctx", [(i, (i + distance) % n) for i in range(n)])


def my_half(other):
    core = lax.rem(lax.axis_index("ctx"), 2)
    return 1 - core if other else core


def columns(index, width):
    return pl.ds(pl.multiple_of(index * width, width), width)


def prep_kv_kernel(other, k_ref, v_ref, *refs):
    *tables, out_ref, k_buf, v_buf, sems = refs
    pick = my_half(other)
    copies = [
        pltpu.make_async_copy(ref.at[:, columns(pick, 2 * HD)], buf, sems.at[i])
        for i, (ref, buf) in enumerate(((k_ref, k_buf), (v_ref, v_buf)))
    ]
    for copy in copies:
        copy.start()
    lane = lax.broadcasted_iota(jnp.int32, (16, LEN), 1)
    info = jnp.full((16, LEN), -1, jnp.int32)
    slot = 0
    for table in tables:
        for col in range(2):
            info = jnp.where(lane == slot, table[0, col], info)
            slot += 1
    out_ref[INFO:, :] = info.astype(jnp.float32).astype(jnp.bfloat16)
    copies[1].wait()
    for pair in range(2):
        out_ref[LEN + pair * HD : LEN + (pair + 1) * HD, :] = v_buf[:, pair * HD : (pair + 1) * HD].T
    copies[0].wait()
    out_ref[:LEN, :] = k_buf[...]


def prep_kv(keys, values, tables, other):
    return pl.pallas_call(
        functools.partial(prep_kv_kernel, other),
        out_shape=jax.ShapeDtypeStruct(CHUNK, jnp.bfloat16),
        in_specs=[ANY, ANY] + [SMEM] * len(tables),
        out_specs=VMEM,
        scratch_shapes=[pltpu.VMEM((LEN, LEN), jnp.bfloat16)] * 2 + [pltpu.SemaphoreType.DMA((2,))],
        compiler_params=pltpu.CompilerParams(vmem_limit_bytes=4 << 20),
        name="prep_kv",
    )(keys, values, *tables)


def prep_q_kernel(other, q_ref, out_ref, q_buf, sems):
    pick = my_half(other)
    pairs = out_ref.shape[0]
    copies = [
        pltpu.make_async_copy(
            q_ref.at[:, columns(pick * pairs + pair, GROUP * HD)], q_buf.at[pair], sems.at[pair]
        )
        for pair in range(pairs)
    ]
    for copy in copies:
        copy.start()
    for pair, copy in enumerate(copies):
        copy.wait()
        for head in range(GROUP):
            out_ref[pair, :, head * LEN : (head + 1) * LEN] = q_buf[
                pair, :, head * HD : (head + 1) * HD
            ].T


def prep_q(queries, other):
    pairs = queries.shape[1] // (2 * GROUP * HD)
    return pl.pallas_call(
        functools.partial(prep_q_kernel, other),
        out_shape=jax.ShapeDtypeStruct((pairs, HD, WIDE), jnp.bfloat16),
        in_specs=[ANY],
        out_specs=VMEM,
        scratch_shapes=[
            pltpu.VMEM((pairs, LEN, GROUP * HD), jnp.bfloat16),
            pltpu.SemaphoreType.DMA((pairs,)),
        ],
        compiler_params=pltpu.CompilerParams(vmem_limit_bytes=4 << 20),
        name="prep_q",
    )(queries)


def merge_kernel(got_ref, full_in, full_ref, sem):
    copy = pltpu.make_async_copy(got_ref, full_ref.at[:, columns(my_half(True), got_ref.shape[1])], sem)
    copy.start()
    copy.wait()


def merge(got, full):
    return pl.pallas_call(
        merge_kernel,
        out_shape=jax.ShapeDtypeStruct(full.shape, full.dtype),
        in_specs=[VMEM, ANY],
        out_specs=ANY,
        scratch_shapes=[pltpu.SemaphoreType.DMA],
        input_output_aliases={1: 0},
        compiler_params=pltpu.CompilerParams(vmem_limit_bytes=4 << 20),
        name="merge",
    )(got, full)


def pair_step(q_ref, chunk_ref, acc_ref, ml_ref, chunk, tile, pair, bounds):
    k_tile = chunk_ref[chunk, :LEN, pl.ds(pl.multiple_of(pair * HD, HD), HD)]
    v_turned = chunk_ref[chunk, pl.ds(pl.multiple_of(LEN + pair * HD, HD), HD), :]
    queries = q_ref[tile, pair]
    peaks = ml_ref[tile, pair, 0]
    totals = ml_ref[tile, pair, 1]
    new_peaks, new_totals, products, fades = [], [], [], []
    for head in range(GROUP):
        lanes = slice(head * LEN, (head + 1) * LEN)
        scores = jnp.dot(k_tile, queries[:, lanes], preferred_element_type=jnp.float32)
        if bounds is not None:
            scores = jnp.where(bounds, scores, MASKED)
        peak = jnp.maximum(peaks[:, lanes], jnp.max(scores, axis=0, keepdims=True))
        weights = jnp.exp2((scores - peak) * COEF)
        fade = jnp.exp2((peaks[:, lanes] - peak) * COEF)
        new_peaks.append(peak)
        new_totals.append(totals[:, lanes] * fade + jnp.sum(weights, axis=0, keepdims=True))
        fades.append(fade)
        products.append(
            jnp.dot(v_turned, weights.astype(jnp.bfloat16), preferred_element_type=jnp.float32)
        )
    for head in range(GROUP):
        lanes = slice(head * LEN, (head + 1) * LEN)
        ml_ref[tile, pair, 0, :, lanes] = new_peaks[head]
        ml_ref[tile, pair, 1, :, lanes] = new_totals[head]
        acc_ref[tile, pair, :, lanes] = acc_ref[tile, pair, :, lanes] * fades[head] + products[head]


def attend_kernel(sources, n_infos, first, last, *refs):
    refs = list(refs)
    take = lambda n: [refs.pop(0) for _ in range(n)]
    count = len(sources)
    info_in = take(n_infos)
    q_in = take(2)
    chunk_in = take(count)
    state_in = [] if first else take(3)
    outs = take(2 if last else 3)
    q_ref, chunk_ref, info_ref = take(3)
    state = acc_ref, ml_ref, best_ref = take(3)
    buffers = take(2) if last else []
    info_sem, q_sem, chunk_sem, state_sem = take(4)
    stretch = lax.axis_index("ctx")
    pairs = acc_ref.shape[1]

    copy_of = pltpu.make_async_copy
    info_copies = [
        copy_of(ref.at[INFO:, :], info_ref.at[i], info_sem.at[i]) for i, ref in enumerate(info_in)
    ]
    state_copies = [
        copy_of(source, target, state_sem.at[i]) for i, (source, target) in enumerate(zip(state_in, state))
    ]
    bulk = [copy_of(q_in[i], q_ref.at[i], q_sem.at[i]) for i in range(2)]
    bulk += [copy_of(chunk_in[i], chunk_ref.at[i], chunk_sem.at[i]) for i in range(count)]
    for copy in info_copies + state_copies[::-1] + bulk:
        copy.start()
    if first:
        acc_ref[...] = jnp.zeros_like(acc_ref)
        ml_ref[:, :, 0] = jnp.full_like(ml_ref[:, :, 0], MASKED)
        ml_ref[:, :, 1] = jnp.zeros_like(ml_ref[:, :, 1])
        best_ref[...] = jnp.full_like(best_ref, -1.0)

    for copy in info_copies + state_copies[2:]:
        copy.wait()
    low, high = [], []
    for tile in range(2):
        for block, found in ((0, low), (1, high)):
            row = 2 * tile + block
            number = (2 * (stretch ^ tile) + block).astype(jnp.float32)
            best = best_ref[row]
            for i in range(n_infos):
                entries = info_ref[i, 0:1, :HD].astype(jnp.float32)
                best = jnp.maximum(best, jnp.where(entries <= number, entries, -1.0))
            best_ref[row] = best
            found.append(jnp.max(best).astype(jnp.int32))

    source_of = [(stretch ^ bits) - back for bits, back in sources]

    def view(source, tile, low_start, high_start):
        where = stretch ^ tile
        first_key, first_query = source * LEN, where * LEN
        low_limit = jnp.maximum(low_start * BLK, first_query - WINDOW + 1)
        seen = (source >= 0) & (source <= where) & (first_key + LEN > low_limit)
        high_limit = jnp.maximum(high_start * BLK, first_query + LEN - WINDOW)
        whole = (source < where) & (first_key >= high_limit)
        return seen, whole

    busy = functools.reduce(
        jnp.logical_or,
        [view(source, tile, low[tile], high[tile])[0] for source in source_of for tile in range(2)],
    )
    for copy in state_copies[:2] + bulk:
        copy.wait()

    def visit(step, _):
        chunk, tile = lax.div(step, 2), lax.rem(step, 2)
        source = source_of[0]
        for i in range(1, count):
            source = jnp.where(chunk == i, source_of[i], source)
        low_start = jnp.where(tile == 0, low[0], low[1])
        high_start = jnp.where(tile == 0, high[0], high[1])
        seen, whole = view(source, tile, low_start, high_start)

        def all_heads(masked):
            bounds = None
            if masked:
                lane = lax.broadcasted_iota(jnp.int32, (1, LEN), 1)
                query_pos = (stretch ^ tile) * LEN + lane
                start = jnp.where(lane < BLK, low_start, high_start) * BLK
                least = jnp.maximum(start, query_pos - (WINDOW - 1))
                key_pos = source * LEN + lax.broadcasted_iota(jnp.int32, (LEN, LEN), 0)
                bounds = (key_pos <= query_pos) & (key_pos >= least)

            def one_pair(pair, _):
                pair_step(q_ref, chunk_ref, acc_ref, ml_ref, chunk, tile, pair, bounds)
                return 0

            lax.fori_loop(0, pairs, one_pair, 0)

        @pl.when(seen & whole)
        def _():
            all_heads(False)

        @pl.when(seen & jnp.logical_not(whole))
        def _():
            all_heads(True)

        return 0

    @pl.when(busy)
    def _():
        lax.fori_loop(0, 2 * count, visit, 0)

    if not last:
        back = [
            copy_of(source, target, state_sem.at[i]) for i, (source, target) in enumerate(zip(state, outs))
        ]
        back[2].start()

        @pl.when(busy | first)
        def _():
            for copy in back[:2]:
                copy.start()
            for copy in back[:2]:
                copy.wait()

        back[2].wait()
        return

    earlier = stretch >= 12
    sinks = (outs[0].at[:, columns(my_half(False), outs[1].shape[1])], outs[1])
    leaving = []
    for tile in (1, 0):
        lane = lax.broadcasted_iota(jnp.int32, (1, WIDE), 1)
        start = jnp.where(lax.rem(lane, LEN) < BLK, low[tile], high[tile])
        active = (start >= 0) | earlier
        for pair in range(pairs):
            scale = jnp.where(active, 1.0 / ml_ref[tile, pair, 1], 0.0)
            for head in range(GROUP):
                lanes = slice(head * LEN, (head + 1) * LEN)
                blended = (acc_ref[tile, pair, :, lanes] * scale[:, lanes]).astype(jnp.bfloat16)
                at = (pair * GROUP + head) * HD
                buffers[tile][:, at : at + HD] = blended.T
        copy = copy_of(buffers[tile], sinks[tile], q_sem.at[tile])
        copy.start()
        leaving.append(copy)
    for copy in leaving:
        copy.wait()


def attend(infos, qs, chunks, sources, state, width=0):
    last = width > 0
    first = state is None
    pairs = qs[0].shape[0]
    args = list(infos) + list(qs) + list(chunks)
    state_shapes = (2, pairs, HD, WIDE), (2, pairs, 2, 1, WIDE), (4, 1, HD)
    aliases = {}
    if not first:
        if not last:
            aliases = {len(args) + i: i for i in range(3)}
        args += list(state)
    scratch = [
        pltpu.VMEM((2,) + qs[0].shape, jnp.bfloat16),
        pltpu.VMEM((len(chunks),) + CHUNK, jnp.bfloat16),
        pltpu.VMEM((max(len(infos), 1), 16, LEN), jnp.bfloat16),
    ] + [pltpu.VMEM(s, jnp.float32) for s in state_shapes]
    if last:
        half = pairs * GROUP * HD
        shapes = [jax.ShapeDtypeStruct((LEN, w), jnp.bfloat16) for w in (width, half)]
        scratch += [pltpu.VMEM((LEN, half), jnp.bfloat16)] * 2
    else:
        shapes = [jax.ShapeDtypeStruct(s, jnp.float32) for s in state_shapes]
    scratch += [pltpu.SemaphoreType.DMA((n,)) for n in (max(len(infos), 1), 2, len(chunks), 3)]
    elements = len(chunks) * 2 * pairs * LEN * WIDE
    return pl.pallas_call(
        functools.partial(attend_kernel, sources, len(infos), first, last),
        out_shape=shapes,
        in_specs=[ANY] * len(args),
        out_specs=[ANY] * len(shapes),
        scratch_shapes=scratch,
        input_output_aliases=aliases,
        cost_estimate=pl.CostEstimate(
            flops=4 * HD * elements, bytes_accessed=6 << 20, transcendentals=elements
        ),
        compiler_params=pltpu.CompilerParams(vmem_limit_bytes=LIMIT),
        name="attend",
    )(*args)


def on_device(queries, keys, values, doc_starts):
    rows, width = queries.shape
    assert rows == LEN and keys.shape[1] == 4 * HD and lax.axis_size("ctx") % 4 == 0
    across = exchanged(doc_starts, 2)
    own = prep_kv(keys, values, (doc_starts,), False)
    a_own = shifted(own, 4)
    send = prep_kv(keys, values, (doc_starts, across), True)
    pair = exchanged(send, 1)
    q_pair = exchanged(prep_q(queries, True), 1)
    qs = (prep_q(queries, False), q_pair)
    a_pair = shifted(pair, 4)
    y_own = exchanged(own, 2)
    y_pair = exchanged(pair, 2)
    b_own = shifted(a_own, 4)
    ya_own = exchanged(a_own, 2)
    b_pair = shifted(a_pair, 4)
    ya_pair = exchanged(a_pair, 2)
    yb_own = exchanged(b_own, 2)
    yb_pair = exchanged(b_pair, 2)
    state = attend((own, pair), qs, (own, pair), ((0, 0), (1, 0)), None)
    state = attend(
        (y_own, a_own, a_pair, ya_own),
        qs,
        (y_own, y_pair, a_own, a_pair, ya_own),
        ((2, 0), (3, 0), (0, 4), (1, 4), (2, 4)),
        state,
    )
    state = attend(
        (b_own, b_pair, yb_own),
        qs,
        (ya_pair, b_own, b_pair, yb_own),
        ((3, 4), (0, 8), (1, 8), (2, 8)),
        state,
    )
    full, out_send = attend((), qs, (yb_pair,), ((3, 8),), state, width)
    return merge(exchanged(out_send, 1), full)


def solution(mesh):
    spec = P(("groups", "ctx"), None)
    return jax.shard_map(
        on_device, mesh=mesh, in_specs=(spec,) * 4, out_specs=spec, check_vma=False
    )
```

```python
import functools
import math

import jax
import jax.numpy as jnp
from jax import lax
from jax.experimental import pallas as pl
from jax.experimental.pallas import tpu as pltpu
from jax.sharding import PartitionSpec as P

HD = 128
WINDOW = 2048
BLK = 128
LEN = 256
GROUP = 4
WIDE = GROUP * LEN
INFO = 2 * LEN
CHUNK = (INFO + 16, LEN)
MASKED = -1e30
COEF = math.log2(math.e) / math.sqrt(HD)

VMEM = pl.BlockSpec(memory_space=pltpu.VMEM)
SMEM = pl.BlockSpec(memory_space=pltpu.SMEM)
ANY = pl.BlockSpec(memory_space=pl.ANY)
LIMIT = 20 << 20


def exchanged(x, bit):
    n = lax.axis_size("ctx")
    return lax.ppermute(x, "ctx", [(i, i ^ bit) for i in range(n)])


def shifted(x, distance):
    n = lax.axis_size("ctx")
    return lax.ppermute(x, "ctx", [(i, (i + distance) % n) for i in range(n)])


def my_half(other):
    core = lax.rem(lax.axis_index("ctx"), 2)
    return 1 - core if other else core


def columns(index, width):
    return pl.ds(pl.multiple_of(index * width, width), width)


def prep_kv_kernel(other, k_ref, v_ref, *refs):
    *tables, out_ref, k_buf, v_buf, sems = refs
    pick = my_half(other)
    copies = [
        pltpu.make_async_copy(ref.at[:, columns(pick, 2 * HD)], buf, sems.at[i])
        for i, (ref, buf) in enumerate(((k_ref, k_buf), (v_ref, v_buf)))
    ]
    for copy in copies:
        copy.start()
    lane = lax.broadcasted_iota(jnp.int32, (16, LEN), 1)
    info = jnp.full((16, LEN), -1, jnp.int32)
    slot = 0
    for table in tables:
        for col in range(2):
            info = jnp.where(lane == slot, table[0, col], info)
            slot += 1
    out_ref[INFO:, :] = info.astype(jnp.float32).astype(jnp.bfloat16)
    copies[1].wait()
    for pair in range(2):
        out_ref[LEN + pair * HD : LEN + (pair + 1) * HD, :] = v_buf[:, pair * HD : (pair + 1) * HD].T
    copies[0].wait()
    out_ref[:LEN, :] = k_buf[...]


def prep_kv(keys, values, tables, other):
    return pl.pallas_call(
        functools.partial(prep_kv_kernel, other),
        out_shape=jax.ShapeDtypeStruct(CHUNK, jnp.bfloat16),
        in_specs=[ANY, ANY] + [SMEM] * len(tables),
        out_specs=VMEM,
        scratch_shapes=[pltpu.VMEM((LEN, LEN), jnp.bfloat16)] * 2 + [pltpu.SemaphoreType.DMA((2,))],
        compiler_params=pltpu.CompilerParams(vmem_limit_bytes=4 << 20 if other else None),
        name="prep_kv",
    )(keys, values, *tables)


def prep_q_kernel(other, q_ref, out_ref, q_buf, sems):
    pick = my_half(other)
    pairs = out_ref.shape[0]
    copies = [
        pltpu.make_async_copy(
            q_ref.at[:, columns(pick * pairs + pair, GROUP * HD)], q_buf.at[pair], sems.at[pair]
        )
        for pair in range(pairs)
    ]
    for copy in copies:
        copy.start()
    for pair, copy in enumerate(copies):
        copy.wait()
        for head in range(GROUP):
            out_ref[pair, :, head * LEN : (head + 1) * LEN] = q_buf[
                pair, :, head * HD : (head + 1) * HD
            ].T


def prep_q(queries, other):
    pairs = queries.shape[1] // (2 * GROUP * HD)
    return pl.pallas_call(
        functools.partial(prep_q_kernel, other),
        out_shape=jax.ShapeDtypeStruct((pairs, HD, WIDE), jnp.bfloat16),
        in_specs=[ANY],
        out_specs=VMEM,
        scratch_shapes=[
            pltpu.VMEM((pairs, LEN, GROUP * HD), jnp.bfloat16),
            pltpu.SemaphoreType.DMA((pairs,)),
        ],
        compiler_params=pltpu.CompilerParams(vmem_limit_bytes=4 << 20),
        name="prep_q",
    )(queries)


def pick_kernel(lower_ref, upper_ref, out_ref, sem):
    second = lax.rem(lax.div(lax.axis_index("ctx"), 2), 2) == 1

    @pl.when(second)
    def _():
        pltpu.make_async_copy(upper_ref, out_ref, sem).start()

    @pl.when(jnp.logical_not(second))
    def _():
        pltpu.make_async_copy(lower_ref, out_ref, sem).start()

    pltpu.make_async_copy(lower_ref, out_ref, sem).wait()


def crossed(lower, upper):
    picked = pl.pallas_call(
        pick_kernel,
        out_shape=jax.ShapeDtypeStruct(lower.shape, lower.dtype),
        in_specs=[ANY] * 2,
        out_specs=VMEM,
        scratch_shapes=[pltpu.SemaphoreType.DMA],
        compiler_params=pltpu.CompilerParams(vmem_limit_bytes=2 << 20),
        name="pick",
    )(lower, upper)
    return exchanged(picked, 2)


def merge_kernel(got_ref, full_in, full_ref, sem):
    copy = pltpu.make_async_copy(got_ref, full_ref.at[:, columns(my_half(True), got_ref.shape[1])], sem)
    copy.start()
    copy.wait()


def merge(got, full):
    return pl.pallas_call(
        merge_kernel,
        out_shape=jax.ShapeDtypeStruct(full.shape, full.dtype),
        in_specs=[VMEM, ANY],
        out_specs=ANY,
        scratch_shapes=[pltpu.SemaphoreType.DMA],
        input_output_aliases={1: 0},
        compiler_params=pltpu.CompilerParams(vmem_limit_bytes=4 << 20),
        name="merge",
    )(got, full)


def pair_step(q_ref, chunk_ref, acc_ref, ml_ref, chunk, tile, pair, bounds):
    k_tile = chunk_ref[chunk, :LEN, pl.ds(pl.multiple_of(pair * HD, HD), HD)]
    v_turned = chunk_ref[chunk, pl.ds(pl.multiple_of(LEN + pair * HD, HD), HD), :]
    queries = q_ref[tile, pair]
    peaks = ml_ref[tile, pair, 0]
    totals = ml_ref[tile, pair, 1]
    lanes = [slice(head * LEN, (head + 1) * LEN) for head in range(GROUP)]
    scores = [
        jnp.dot(k_tile, queries[:, at], preferred_element_type=jnp.float32) for at in lanes
    ]
    if bounds is not None:
        scores = [jnp.where(bounds, s, MASKED) for s in scores]
    new = [
        jnp.maximum(peaks[:, at], jnp.max(s, axis=0, keepdims=True)) for at, s in zip(lanes, scores)
    ]
    weights = [jnp.exp2((s - peak) * COEF) for s, peak in zip(scores, new)]
    products = [
        jnp.dot(v_turned, w.astype(jnp.bfloat16), preferred_element_type=jnp.float32) for w in weights
    ]
    fades = [jnp.exp2((peaks[:, at] - peak) * COEF) for at, peak in zip(lanes, new)]
    sums = [jnp.sum(w, axis=0, keepdims=True) for w in weights]
    for head, at in enumerate(lanes):
        ml_ref[tile, pair, 0, :, at] = new[head]
        ml_ref[tile, pair, 1, :, at] = totals[:, at] * fades[head] + sums[head]
        acc_ref[tile, pair, :, at] = acc_ref[tile, pair, :, at] * fades[head] + products[head]


def attend_kernel(sources, n_infos, first, last, *refs):
    refs = list(refs)
    take = lambda n: [refs.pop(0) for _ in range(n)]
    count = len(sources)
    info_in = take(n_infos)
    q_in = take(2)
    chunk_in = take(count)
    state_in = [] if first else take(3)
    outs = take(2 if last else 3)
    q_ref, chunk_ref, info_ref = take(3)
    state = acc_ref, ml_ref, best_ref = take(3)
    buffers = take(2) if last else []
    info_sem, q_sem, chunk_sem, state_sem = take(4)
    stretch = lax.axis_index("ctx")
    pairs = acc_ref.shape[1]

    copy_of = pltpu.make_async_copy
    info_copies = [
        copy_of(ref.at[INFO:, :], info_ref.at[i], info_sem.at[i]) for i, ref in enumerate(info_in)
    ]
    state_copies = [
        copy_of(source, target, state_sem.at[i]) for i, (source, target) in enumerate(zip(state_in, state))
    ]
    bulk = [copy_of(q_in[i], q_ref.at[i], q_sem.at[i]) for i in range(2)]
    bulk += [copy_of(chunk_in[i], chunk_ref.at[i], chunk_sem.at[i]) for i in range(count)]
    for copy in info_copies + state_copies[::-1] + bulk:
        copy.start()
    if first:
        acc_ref[...] = jnp.zeros_like(acc_ref)
        ml_ref[:, :, 0] = jnp.full_like(ml_ref[:, :, 0], MASKED)
        ml_ref[:, :, 1] = jnp.zeros_like(ml_ref[:, :, 1])
        best_ref[...] = jnp.full_like(best_ref, -1.0)

    for copy in info_copies + state_copies[2:]:
        copy.wait()
    low, high = [], []
    for tile in range(2):
        for block, found in ((0, low), (1, high)):
            row = 2 * tile + block
            number = (2 * (stretch ^ tile) + block).astype(jnp.float32)
            best = best_ref[row]
            for i in range(n_infos):
                entries = info_ref[i, 0:1, :HD].astype(jnp.float32)
                best = jnp.maximum(best, jnp.where(entries <= number, entries, -1.0))
            best_ref[row] = best
            found.append(jnp.max(best).astype(jnp.int32))

    second = lax.rem(lax.div(stretch, 2), 2) == 1
    source_of = [
        (stretch ^ bits) - jnp.where(second, upper, lower) for bits, lower, upper in sources
    ]

    def view(source, tile, low_start, high_start):
        where = stretch ^ tile
        first_key, first_query = source * LEN, where * LEN
        low_limit = jnp.maximum(low_start * BLK, first_query - WINDOW + 1)
        seen = (source >= 0) & (source <= where) & (first_key + LEN > low_limit)
        high_limit = jnp.maximum(high_start * BLK, first_query + LEN - WINDOW)
        whole = (source < where) & (first_key >= high_limit)
        return seen, whole

    busy = functools.reduce(
        jnp.logical_or,
        [view(source, tile, low[tile], high[tile])[0] for source in source_of for tile in range(2)],
    )
    for copy in state_copies[:2] + bulk:
        copy.wait()

    def visit(step, _):
        chunk, tile = lax.div(step, 2), lax.rem(step, 2)
        source = source_of[0]
        for i in range(1, count):
            source = jnp.where(chunk == i, source_of[i], source)
        low_start = jnp.where(tile == 0, low[0], low[1])
        high_start = jnp.where(tile == 0, high[0], high[1])
        seen, whole = view(source, tile, low_start, high_start)

        def all_heads(masked):
            bounds = None
            if masked:
                lane = lax.broadcasted_iota(jnp.int32, (1, LEN), 1)
                query_pos = (stretch ^ tile) * LEN + lane
                start = jnp.where(lane < BLK, low_start, high_start) * BLK
                least = jnp.maximum(start, query_pos - (WINDOW - 1))
                key_pos = source * LEN + lax.broadcasted_iota(jnp.int32, (LEN, LEN), 0)
                bounds = (key_pos <= query_pos) & (key_pos >= least)

            def one_pair(pair, _):
                pair_step(q_ref, chunk_ref, acc_ref, ml_ref, chunk, tile, pair, bounds)
                return 0

            lax.fori_loop(0, pairs, one_pair, 0)

        @pl.when(seen & whole)
        def _():
            all_heads(False)

        @pl.when(seen & jnp.logical_not(whole))
        def _():
            all_heads(True)

        return 0

    @pl.when(busy)
    def _():
        lax.fori_loop(0, 2 * count, visit, 0)

    if not last:
        back = [
            copy_of(source, target, state_sem.at[i]) for i, (source, target) in enumerate(zip(state, outs))
        ]
        back[2].start()

        @pl.when(busy | first)
        def _():
            for copy in back[:2]:
                copy.start()
            for copy in back[:2]:
                copy.wait()

        back[2].wait()
        return

    sinks = (outs[0].at[:, columns(my_half(False), outs[1].shape[1])], outs[1])
    leaving = []
    for tile in (1, 0):
        lane = lax.broadcasted_iota(jnp.int32, (1, WIDE), 1)
        start = jnp.where(lax.rem(lane, LEN) < BLK, low[tile], high[tile])
        active = (start >= 0) | ((stretch ^ tile) >= 1)
        for pair in range(pairs):
            scale = jnp.where(active, 1.0 / ml_ref[tile, pair, 1], 0.0)
            for head in range(GROUP):
                lanes = slice(head * LEN, (head + 1) * LEN)
                blended = (acc_ref[tile, pair, :, lanes] * scale[:, lanes]).astype(jnp.bfloat16)
                at = (pair * GROUP + head) * HD
                buffers[tile][:, at : at + HD] = blended.T
        copy = copy_of(buffers[tile], sinks[tile], q_sem.at[tile])
        copy.start()
        leaving.append(copy)
    for copy in leaving:
        copy.wait()


def attend(infos, qs, chunks, sources, state, width=0):
    last = width > 0
    first = state is None
    pairs = qs[0].shape[0]
    args = list(infos) + list(qs) + list(chunks)
    state_shapes = (2, pairs, HD, WIDE), (2, pairs, 2, 1, WIDE), (4, 1, HD)
    aliases = {}
    if not first:
        if not last:
            aliases = {len(args) + i: i for i in range(3)}
        args += list(state)
    scratch = [
        pltpu.VMEM((2,) + qs[0].shape, jnp.bfloat16),
        pltpu.VMEM((len(chunks),) + CHUNK, jnp.bfloat16),
        pltpu.VMEM((max(len(infos), 1), 16, LEN), jnp.bfloat16),
    ] + [pltpu.VMEM(s, jnp.float32) for s in state_shapes]
    if last:
        half = pairs * GROUP * HD
        shapes = [jax.ShapeDtypeStruct((LEN, w), jnp.bfloat16) for w in (width, half)]
        scratch += [pltpu.VMEM((LEN, half), jnp.bfloat16)] * 2
    else:
        shapes = [jax.ShapeDtypeStruct(s, jnp.float32) for s in state_shapes]
    scratch += [pltpu.SemaphoreType.DMA((n,)) for n in (max(len(infos), 1), 2, len(chunks), 3)]
    elements = len(chunks) * 2 * pairs * LEN * WIDE
    return pl.pallas_call(
        functools.partial(attend_kernel, sources, len(infos), first, last),
        out_shape=shapes,
        in_specs=[ANY] * len(args),
        out_specs=[ANY] * len(shapes),
        scratch_shapes=scratch,
        input_output_aliases=aliases,
        cost_estimate=pl.CostEstimate(
            flops=4 * HD * elements, bytes_accessed=6 << 20, transcendentals=elements
        ),
        compiler_params=pltpu.CompilerParams(vmem_limit_bytes=LIMIT),
        name="attend",
    )(*args)


def steps(queries, keys, values, doc_starts):
    rows, width = queries.shape
    assert rows == LEN and keys.shape[1] == 4 * HD and lax.axis_size("ctx") % 4 == 0
    own = prep_kv(keys, values, (doc_starts,), False)
    a_own = shifted(own, 4)
    across = exchanged(doc_starts, 2)
    q_send = prep_q(queries, True)
    q_pair = exchanged(q_send, 1)
    send = prep_kv(keys, values, (doc_starts, across), True)
    pair = exchanged(send, 1)
    qs = (prep_q(queries, False), q_pair)
    a_pair = shifted(pair, 4)
    x_own = crossed(own, a_own)
    b_own = shifted(a_own, 4)
    state = attend((own, pair), qs, (own, pair), ((0, 0, 0), (1, 0, 0)), None)
    x_pair = crossed(pair, a_pair)
    b_pair = shifted(a_pair, 4)
    state = attend(
        (a_own, a_pair, x_own),
        qs,
        (a_own, a_pair, x_own),
        ((0, 4, 4), (1, 4, 4), (2, 4, 0)),
        state,
    )
    xb_own = crossed(a_own, b_own)
    xb_pair = crossed(a_pair, b_pair)
    state = attend(
        (b_own, b_pair, xb_own),
        qs,
        (x_pair, b_own, b_pair, xb_own),
        ((3, 4, 0), (0, 8, 8), (1, 8, 8), (2, 8, 4)),
        state,
    )
    full, out_send = attend((), qs, (xb_pair,), ((3, 8, 4),), state, width)
    return merge(exchanged(out_send, 1), full)


def solution(mesh):
    spec = P(("groups", "ctx"), None)
    return jax.shard_map(steps, mesh=mesh, in_specs=(spec,) * 4, out_specs=spec, check_vma=False)
```

```python
import functools
import math

import jax
import jax.numpy as jnp
from jax import lax
from jax.experimental import pallas as pl
from jax.experimental.pallas import tpu as pltpu
from jax.sharding import PartitionSpec as P

HD = 128
WINDOW = 2048
BLK = 128
LEN = 256
GROUP = 4
WIDE = GROUP * LEN
INFO = 2 * LEN
CHUNK = (INFO + 16, LEN)
MASKED = -1e30
COEF = math.log2(math.e) / math.sqrt(HD)

VMEM = pl.BlockSpec(memory_space=pltpu.VMEM)
SMEM = pl.BlockSpec(memory_space=pltpu.SMEM)
ANY = pl.BlockSpec(memory_space=pl.ANY)
LIMIT = 20 << 20


def exchanged(x, bit):
    n = lax.axis_size("ctx")
    return lax.ppermute(x, "ctx", [(i, i ^ bit) for i in range(n)])


def shifted(x, distance):
    n = lax.axis_size("ctx")
    return lax.ppermute(x, "ctx", [(i, (i + distance) % n) for i in range(n)])


def my_half(other):
    core = lax.rem(lax.axis_index("ctx"), 2)
    return 1 - core if other else core


def columns(index, width):
    return pl.ds(pl.multiple_of(index * width, width), width)


def prep_kv_kernel(other, count, k_ref, v_ref, *refs):
    table_refs, (out_ref, k_buf, v_buf, turned, info_buf) = refs[:count], refs[count : count + 5]
    tables, sems, out_sems = refs[count + 5 :]
    pick = my_half(other)
    rows = LEN // 2
    fetch = pltpu.make_async_copy
    starts = [fetch(ref, tables.at[i], sems.at[4 + i]) for i, ref in enumerate(table_refs)]
    v_in = [
        fetch(v_ref.at[i * rows : (i + 1) * rows, columns(pick, 2 * HD)], v_buf.at[i], sems.at[i])
        for i in range(2)
    ]
    k_in = [
        fetch(k_ref.at[i * rows : (i + 1) * rows, columns(pick, 2 * HD)], k_buf.at[i], sems.at[2 + i])
        for i in range(2)
    ]
    for copy in starts + v_in + k_in:
        copy.start()
    leaving = []

    def leave(source, first, last):
        copy = fetch(source, out_ref.at[first:last], out_sems.at[len(leaving)])
        copy.start()
        leaving.append(copy)

    for copy in starts:
        copy.wait()
    lane = lax.broadcasted_iota(jnp.int32, (16, LEN), 1)
    info = jnp.full((16, LEN), -1, jnp.int32)
    for i in range(count):
        for col in range(2):
            info = jnp.where(lane == 2 * i + col, tables[i, 0, col], info)
    info_buf[...] = info.astype(jnp.float32).astype(jnp.bfloat16)
    leave(info_buf, INFO, INFO + 16)
    for i, copy in enumerate(v_in):
        copy.wait()
        for pair in range(2):
            turned[pair * HD : (pair + 1) * HD, i * rows : (i + 1) * rows] = v_buf[
                i, :, pair * HD : (pair + 1) * HD
            ].T
    leave(turned, LEN, INFO)
    for i, copy in enumerate(k_in):
        copy.wait()
        leave(k_buf.at[i], i * rows, (i + 1) * rows)
    for copy in leaving:
        copy.wait()


def prep_kv(keys, values, tables, other):
    return pl.pallas_call(
        functools.partial(prep_kv_kernel, other, len(tables)),
        out_shape=jax.ShapeDtypeStruct(CHUNK, jnp.bfloat16),
        in_specs=[ANY] * (2 + len(tables)),
        out_specs=ANY,
        scratch_shapes=[
            pltpu.VMEM((2, LEN // 2, LEN), jnp.bfloat16),
            pltpu.VMEM((2, LEN // 2, LEN), jnp.bfloat16),
            pltpu.VMEM((LEN, LEN), jnp.bfloat16),
            pltpu.VMEM((16, LEN), jnp.bfloat16),
            pltpu.SMEM((len(tables), 1, 2), jnp.int32),
            pltpu.SemaphoreType.DMA((4 + len(tables),)),
            pltpu.SemaphoreType.DMA((4,)),
        ],
        name="prep_kv",
    )(keys, values, *tables)


def prep_q_kernel(other, q_ref, out_ref, q_buf, sems):
    pick = my_half(other)
    pairs = out_ref.shape[0]
    copies = [
        pltpu.make_async_copy(
            q_ref.at[:, columns(pick * pairs + pair, GROUP * HD)], q_buf.at[pair], sems.at[pair]
        )
        for pair in range(pairs)
    ]
    for copy in copies:
        copy.start()
    for pair, copy in enumerate(copies):
        copy.wait()
        for head in range(GROUP):
            out_ref[pair, :, head * LEN : (head + 1) * LEN] = q_buf[
                pair, :, head * HD : (head + 1) * HD
            ].T


def prep_q(queries, other):
    pairs = queries.shape[1] // (2 * GROUP * HD)
    return pl.pallas_call(
        functools.partial(prep_q_kernel, other),
        out_shape=jax.ShapeDtypeStruct((pairs, HD, WIDE), jnp.bfloat16),
        in_specs=[ANY],
        out_specs=VMEM,
        scratch_shapes=[
            pltpu.VMEM((pairs, LEN, GROUP * HD), jnp.bfloat16),
            pltpu.SemaphoreType.DMA((pairs,)),
        ],
        compiler_params=pltpu.CompilerParams(vmem_limit_bytes=4 << 20),
        name="prep_q",
    )(queries)


def pick_kernel(lower_ref, upper_ref, out_ref, sem):
    second = lax.rem(lax.div(lax.axis_index("ctx"), 2), 2) == 1

    @pl.when(second)
    def _():
        pltpu.make_async_copy(upper_ref, out_ref, sem).start()

    @pl.when(jnp.logical_not(second))
    def _():
        pltpu.make_async_copy(lower_ref, out_ref, sem).start()

    pltpu.make_async_copy(lower_ref, out_ref, sem).wait()


def crossed(lower, upper):
    picked = pl.pallas_call(
        pick_kernel,
        out_shape=jax.ShapeDtypeStruct(lower.shape, lower.dtype),
        in_specs=[ANY] * 2,
        out_specs=VMEM,
        scratch_shapes=[pltpu.SemaphoreType.DMA],
        compiler_params=pltpu.CompilerParams(vmem_limit_bytes=2 << 20),
        name="pick",
    )(lower, upper)
    return exchanged(picked, 2)


def merge_kernel(got_ref, full_in, full_ref, sem):
    copy = pltpu.make_async_copy(got_ref, full_ref.at[:, columns(my_half(True), got_ref.shape[1])], sem)
    copy.start()
    copy.wait()


def merge(got, full):
    return pl.pallas_call(
        merge_kernel,
        out_shape=jax.ShapeDtypeStruct(full.shape, full.dtype),
        in_specs=[VMEM, ANY],
        out_specs=ANY,
        scratch_shapes=[pltpu.SemaphoreType.DMA],
        input_output_aliases={1: 0},
        compiler_params=pltpu.CompilerParams(vmem_limit_bytes=4 << 20),
        name="merge",
    )(got, full)


def pair_step(q_ref, chunk_ref, acc_ref, ml_ref, chunk, tile, pair, bounds):
    k_tile = chunk_ref[chunk, :LEN, pl.ds(pl.multiple_of(pair * HD, HD), HD)]
    v_turned = chunk_ref[chunk, pl.ds(pl.multiple_of(LEN + pair * HD, HD), HD), :]
    queries = q_ref[tile, pair]
    peaks = ml_ref[tile, pair, 0]
    totals = ml_ref[tile, pair, 1]
    lanes = [slice(head * LEN, (head + 1) * LEN) for head in range(GROUP)]
    scores = [
        jnp.dot(k_tile, queries[:, at], preferred_element_type=jnp.float32) for at in lanes
    ]
    if bounds is not None:
        scores = [jnp.where(bounds, s, MASKED) for s in scores]
    new = [
        jnp.maximum(peaks[:, at], jnp.max(s, axis=0, keepdims=True)) for at, s in zip(lanes, scores)
    ]
    weights = [jnp.exp2((s - peak) * COEF) for s, peak in zip(scores, new)]
    products = [
        jnp.dot(v_turned, w.astype(jnp.bfloat16), preferred_element_type=jnp.float32) for w in weights
    ]
    fades = [jnp.exp2((peaks[:, at] - peak) * COEF) for at, peak in zip(lanes, new)]
    sums = [jnp.sum(w, axis=0, keepdims=True) for w in weights]
    for head, at in enumerate(lanes):
        ml_ref[tile, pair, 0, :, at] = new[head]
        ml_ref[tile, pair, 1, :, at] = totals[:, at] * fades[head] + sums[head]
        acc_ref[tile, pair, :, at] = acc_ref[tile, pair, :, at] * fades[head] + products[head]


def attend_kernel(sources, n_infos, first, last, *refs):
    refs = list(refs)
    take = lambda n: [refs.pop(0) for _ in range(n)]
    count = len(sources)
    info_in = take(n_infos)
    q_in = take(2)
    chunk_in = take(count)
    state_in = [] if first else take(3)
    outs = take(2 if last else 3)
    q_ref, chunk_ref, info_ref = take(3)
    state = acc_ref, ml_ref, best_ref = take(3)
    buffers = take(2) if last else []
    info_sem, q_sem, chunk_sem, state_sem = take(4)
    stretch = lax.axis_index("ctx")
    pairs = acc_ref.shape[1]

    copy_of = pltpu.make_async_copy
    info_copies = [
        copy_of(ref.at[INFO:, :], info_ref.at[i], info_sem.at[i]) for i, ref in enumerate(info_in)
    ]
    state_copies = [
        copy_of(source, target, state_sem.at[i]) for i, (source, target) in enumerate(zip(state_in, state))
    ]
    bulk = [copy_of(q_in[i], q_ref.at[i], q_sem.at[i]) for i in range(2)]
    bulk += [copy_of(chunk_in[i], chunk_ref.at[i], chunk_sem.at[i]) for i in range(count)]
    for copy in info_copies + state_copies[::-1] + bulk:
        copy.start()
    if first:
        acc_ref[...] = jnp.zeros_like(acc_ref)
        ml_ref[:, :, 0] = jnp.full_like(ml_ref[:, :, 0], MASKED)
        ml_ref[:, :, 1] = jnp.zeros_like(ml_ref[:, :, 1])
        best_ref[...] = jnp.full_like(best_ref, -1.0)

    for copy in info_copies + state_copies[2:]:
        copy.wait()
    low, high = [], []
    for tile in range(2):
        for block, found in ((0, low), (1, high)):
            row = 2 * tile + block
            number = (2 * (stretch ^ tile) + block).astype(jnp.float32)
            best = best_ref[row]
            for i in range(n_infos):
                entries = info_ref[i, 0:1, :HD].astype(jnp.float32)
                best = jnp.maximum(best, jnp.where(entries <= number, entries, -1.0))
            best_ref[row] = best
            found.append(jnp.max(best).astype(jnp.int32))

    second = lax.rem(lax.div(stretch, 2), 2) == 1
    source_of = [
        (stretch ^ bits) - jnp.where(second, upper, lower) for bits, lower, upper in sources
    ]

    def view(source, tile, low_start, high_start):
        where = stretch ^ tile
        first_key, first_query = source * LEN, where * LEN
        low_limit = jnp.maximum(low_start * BLK, first_query - WINDOW + 1)
        seen = (source >= 0) & (source <= where) & (first_key + LEN > low_limit)
        high_limit = jnp.maximum(high_start * BLK, first_query + LEN - WINDOW)
        whole = (source < where) & (first_key >= high_limit)
        return seen, whole

    busy = functools.reduce(
        jnp.logical_or,
        [view(source, tile, low[tile], high[tile])[0] for source in source_of for tile in range(2)],
    )
    for copy in state_copies[:2] + bulk:
        copy.wait()

    def visit(step, _):
        chunk, tile = lax.div(step, 2), lax.rem(step, 2)
        source = source_of[0]
        for i in range(1, count):
            source = jnp.where(chunk == i, source_of[i], source)
        low_start = jnp.where(tile == 0, low[0], low[1])
        high_start = jnp.where(tile == 0, high[0], high[1])
        seen, whole = view(source, tile, low_start, high_start)

        def all_heads(masked):
            bounds = None
            if masked:
                lane = lax.broadcasted_iota(jnp.int32, (1, LEN), 1)
                query_pos = (stretch ^ tile) * LEN + lane
                start = jnp.where(lane < BLK, low_start, high_start) * BLK
                least = jnp.maximum(start, query_pos - (WINDOW - 1))
                key_pos = source * LEN + lax.broadcasted_iota(jnp.int32, (LEN, LEN), 0)
                bounds = (key_pos <= query_pos) & (key_pos >= least)

            def one_pair(pair, _):
                pair_step(q_ref, chunk_ref, acc_ref, ml_ref, chunk, tile, pair, bounds)
                return 0

            lax.fori_loop(0, pairs, one_pair, 0)

        @pl.when(seen & whole)
        def _():
            all_heads(False)

        @pl.when(seen & jnp.logical_not(whole))
        def _():
            all_heads(True)

        return 0

    @pl.when(busy)
    def _():
        lax.fori_loop(0, 2 * count, visit, 0)

    if not last:
        back = [
            copy_of(source, target, state_sem.at[i]) for i, (source, target) in enumerate(zip(state, outs))
        ]
        back[2].start()

        @pl.when(busy | first)
        def _():
            for copy in back[:2]:
                copy.start()
            for copy in back[:2]:
                copy.wait()

        back[2].wait()
        return

    sinks = (outs[0].at[:, columns(my_half(False), outs[1].shape[1])], outs[1])
    leaving = []
    for tile in (1, 0):
        lane = lax.broadcasted_iota(jnp.int32, (1, WIDE), 1)
        start = jnp.where(lax.rem(lane, LEN) < BLK, low[tile], high[tile])
        active = (start >= 0) | ((stretch ^ tile) >= 1)
        for pair in range(pairs):
            scale = jnp.where(active, 1.0 / ml_ref[tile, pair, 1], 0.0)
            for head in range(GROUP):
                lanes = slice(head * LEN, (head + 1) * LEN)
                blended = (acc_ref[tile, pair, :, lanes] * scale[:, lanes]).astype(jnp.bfloat16)
                at = (pair * GROUP + head) * HD
                buffers[tile][:, at : at + HD] = blended.T
        copy = copy_of(buffers[tile], sinks[tile], q_sem.at[tile])
        copy.start()
        leaving.append(copy)
    for copy in leaving:
        copy.wait()


def attend(infos, qs, chunks, sources, state, width=0):
    last = width > 0
    first = state is None
    pairs = qs[0].shape[0]
    args = list(infos) + list(qs) + list(chunks)
    state_shapes = (2, pairs, HD, WIDE), (2, pairs, 2, 1, WIDE), (4, 1, HD)
    aliases = {}
    if not first:
        if not last:
            aliases = {len(args) + i: i for i in range(3)}
        args += list(state)
    scratch = [
        pltpu.VMEM((2,) + qs[0].shape, jnp.bfloat16),
        pltpu.VMEM((len(chunks),) + CHUNK, jnp.bfloat16),
        pltpu.VMEM((max(len(infos), 1), 16, LEN), jnp.bfloat16),
    ] + [pltpu.VMEM(s, jnp.float32) for s in state_shapes]
    if last:
        half = pairs * GROUP * HD
        shapes = [jax.ShapeDtypeStruct((LEN, w), jnp.bfloat16) for w in (width, half)]
        scratch += [pltpu.VMEM((LEN, half), jnp.bfloat16)] * 2
    else:
        shapes = [jax.ShapeDtypeStruct(s, jnp.float32) for s in state_shapes]
    scratch += [pltpu.SemaphoreType.DMA((n,)) for n in (max(len(infos), 1), 2, len(chunks), 3)]
    elements = len(chunks) * 2 * pairs * LEN * WIDE
    return pl.pallas_call(
        functools.partial(attend_kernel, sources, len(infos), first, last),
        out_shape=shapes,
        in_specs=[ANY] * len(args),
        out_specs=[ANY] * len(shapes),
        scratch_shapes=scratch,
        input_output_aliases=aliases,
        cost_estimate=pl.CostEstimate(
            flops=4 * HD * elements, bytes_accessed=6 << 20, transcendentals=elements
        ),
        compiler_params=pltpu.CompilerParams(vmem_limit_bytes=LIMIT),
        name="attend",
    )(*args)


def steps(queries, keys, values, doc_starts):
    rows, width = queries.shape
    assert rows == LEN and keys.shape[1] == 4 * HD and lax.axis_size("ctx") % 4 == 0
    own = prep_kv(keys, values, (doc_starts,), False)
    a_own = shifted(own, 4)
    across = exchanged(doc_starts, 2)
    q_send = prep_q(queries, True)
    q_pair = exchanged(q_send, 1)
    send = prep_kv(keys, values, (doc_starts, across), True)
    pair = exchanged(send, 1)
    qs = (prep_q(queries, False), q_pair)
    a_pair = shifted(pair, 4)
    x_own = crossed(own, a_own)
    b_own = shifted(a_own, 4)
    state = attend((own, pair), qs, (own, pair), ((0, 0, 0), (1, 0, 0)), None)
    x_pair = crossed(pair, a_pair)
    b_pair = shifted(a_pair, 4)
    state = attend((a_own, a_pair, x_own), qs, (a_own,), ((0, 4, 4),), state)
    xb_own = crossed(a_own, b_own)
    state = attend((), qs, (a_pair, x_own), ((1, 4, 4), (2, 4, 0)), state)
    xb_pair = crossed(a_pair, b_pair)
    state = attend((), qs, (x_pair,), ((3, 4, 0),), state)
    state = attend(
        (b_own, b_pair, xb_own),
        qs,
        (b_own, b_pair, xb_own),
        ((0, 8, 8), (1, 8, 8), (2, 8, 4)),
        state,
    )
    full, out_send = attend((), qs, (xb_pair,), ((3, 8, 4),), state, width)
    return merge(exchanged(out_send, 1), full)


def solution(mesh):
    spec = P(("groups", "ctx"), None)
    return jax.shard_map(steps, mesh=mesh, in_specs=(spec,) * 4, out_specs=spec, check_vma=False)
```

```python
import functools
import math

import jax
import jax.numpy as jnp
from jax import lax
from jax.experimental import pallas as pl
from jax.experimental.pallas import tpu as pltpu
from jax.sharding import PartitionSpec as P

HD = 128
WINDOW = 2048
BLK = 128
LEN = 256
GROUP = 4
WIDE = GROUP * LEN
INFO = 2 * LEN
CHUNK = (INFO + 16, LEN)
MASKED = -1e30
COEF = math.log2(math.e) / math.sqrt(HD)

VMEM = pl.BlockSpec(memory_space=pltpu.VMEM)
SMEM = pl.BlockSpec(memory_space=pltpu.SMEM)
ANY = pl.BlockSpec(memory_space=pl.ANY)
LIMIT = 20 << 20


def exchanged(x, bit):
    n = lax.axis_size("ctx")
    return lax.ppermute(x, "ctx", [(i, i ^ bit) for i in range(n)])


def shifted(x, distance):
    n = lax.axis_size("ctx")
    return lax.ppermute(x, "ctx", [(i, (i + distance) % n) for i in range(n)])


def my_half(other):
    core = lax.rem(lax.axis_index("ctx"), 2)
    return 1 - core if other else core


def columns(index, width):
    return pl.ds(pl.multiple_of(index * width, width), width)


def prep_kv_kernel(other, count, k_ref, v_ref, *refs):
    table_refs, (out_ref, k_buf, v_buf, turned, info_buf) = refs[:count], refs[count : count + 5]
    tables, sems, out_sems = refs[count + 5 :]
    pick = my_half(other)
    rows = LEN // 2
    fetch = pltpu.make_async_copy
    starts = [fetch(ref, tables.at[i], sems.at[4 + i]) for i, ref in enumerate(table_refs)]
    v_in = [
        fetch(v_ref.at[i * rows : (i + 1) * rows, columns(pick, 2 * HD)], v_buf.at[i], sems.at[i])
        for i in range(2)
    ]
    k_in = [
        fetch(k_ref.at[i * rows : (i + 1) * rows, columns(pick, 2 * HD)], k_buf.at[i], sems.at[2 + i])
        for i in range(2)
    ]
    for copy in starts + v_in + k_in:
        copy.start()
    leaving = []

    def leave(source, first, last):
        copy = fetch(source, out_ref.at[first:last], out_sems.at[len(leaving)])
        copy.start()
        leaving.append(copy)

    for copy in starts:
        copy.wait()
    lane = lax.broadcasted_iota(jnp.int32, (16, LEN), 1)
    info = jnp.full((16, LEN), -1, jnp.int32)
    for i in range(count):
        for col in range(2):
            info = jnp.where(lane == 2 * i + col, tables[i, 0, col], info)
    info_buf[...] = info.astype(jnp.float32).astype(jnp.bfloat16)
    leave(info_buf, INFO, INFO + 16)
    for i, copy in enumerate(v_in):
        copy.wait()
        for pair in range(2):
            turned[pair * HD : (pair + 1) * HD, i * rows : (i + 1) * rows] = v_buf[
                i, :, pair * HD : (pair + 1) * HD
            ].T
    leave(turned, LEN, INFO)
    for i, copy in enumerate(k_in):
        copy.wait()
        leave(k_buf.at[i], i * rows, (i + 1) * rows)
    for copy in leaving:
        copy.wait()


def prep_kv(keys, values, tables, other):
    return pl.pallas_call(
        functools.partial(prep_kv_kernel, other, len(tables)),
        out_shape=jax.ShapeDtypeStruct(CHUNK, jnp.bfloat16),
        in_specs=[ANY] * (2 + len(tables)),
        out_specs=ANY,
        scratch_shapes=[
            pltpu.VMEM((2, LEN // 2, LEN), jnp.bfloat16),
            pltpu.VMEM((2, LEN // 2, LEN), jnp.bfloat16),
            pltpu.VMEM((LEN, LEN), jnp.bfloat16),
            pltpu.VMEM((16, LEN), jnp.bfloat16),
            pltpu.SMEM((len(tables), 1, 2), jnp.int32),
            pltpu.SemaphoreType.DMA((4 + len(tables),)),
            pltpu.SemaphoreType.DMA((4,)),
        ],
        name="prep_kv",
    )(keys, values, *tables)


def prep_q_kernel(other, q_ref, out_ref, q_buf, sems):
    pick = my_half(other)
    pairs = out_ref.shape[0]
    copies = [
        pltpu.make_async_copy(
            q_ref.at[:, columns(pick * pairs + pair, GROUP * HD)], q_buf.at[pair], sems.at[pair]
        )
        for pair in range(pairs)
    ]
    for copy in copies:
        copy.start()
    for pair, copy in enumerate(copies):
        copy.wait()
        for head in range(GROUP):
            out_ref[pair, :, head * LEN : (head + 1) * LEN] = q_buf[
                pair, :, head * HD : (head + 1) * HD
            ].T


def prep_q(queries, other):
    pairs = queries.shape[1] // (2 * GROUP * HD)
    return pl.pallas_call(
        functools.partial(prep_q_kernel, other),
        out_shape=jax.ShapeDtypeStruct((pairs, HD, WIDE), jnp.bfloat16),
        in_specs=[ANY],
        out_specs=VMEM,
        scratch_shapes=[
            pltpu.VMEM((pairs, LEN, GROUP * HD), jnp.bfloat16),
            pltpu.SemaphoreType.DMA((pairs,)),
        ],
        compiler_params=pltpu.CompilerParams(vmem_limit_bytes=4 << 20),
        name="prep_q",
    )(queries)


def pick_kernel(lower_ref, upper_ref, out_ref, sem):
    second = lax.rem(lax.div(lax.axis_index("ctx"), 2), 2) == 1

    @pl.when(second)
    def _():
        pltpu.make_async_copy(upper_ref, out_ref, sem).start()

    @pl.when(jnp.logical_not(second))
    def _():
        pltpu.make_async_copy(lower_ref, out_ref, sem).start()

    pltpu.make_async_copy(lower_ref, out_ref, sem).wait()


def crossed(lower, upper):
    picked = pl.pallas_call(
        pick_kernel,
        out_shape=jax.ShapeDtypeStruct(lower.shape, lower.dtype),
        in_specs=[ANY] * 2,
        out_specs=VMEM,
        scratch_shapes=[pltpu.SemaphoreType.DMA],
        compiler_params=pltpu.CompilerParams(vmem_limit_bytes=2 << 20),
        name="pick",
    )(lower, upper)
    return exchanged(picked, 2)


def merge_kernel(got_ref, full_in, full_ref, sem):
    copy = pltpu.make_async_copy(got_ref, full_ref.at[:, columns(my_half(True), got_ref.shape[1])], sem)
    copy.start()
    copy.wait()


def merge(got, full):
    return pl.pallas_call(
        merge_kernel,
        out_shape=jax.ShapeDtypeStruct(full.shape, full.dtype),
        in_specs=[VMEM, ANY],
        out_specs=ANY,
        scratch_shapes=[pltpu.SemaphoreType.DMA],
        input_output_aliases={1: 0},
        compiler_params=pltpu.CompilerParams(vmem_limit_bytes=4 << 20),
        name="merge",
    )(got, full)


def pair_step(q_ref, chunk_ref, acc_ref, ml_ref, chunk, tile, pair, bounds):
    k_tile = chunk_ref[chunk, :LEN, pl.ds(pl.multiple_of(pair * HD, HD), HD)]
    v_turned = chunk_ref[chunk, pl.ds(pl.multiple_of(LEN + pair * HD, HD), HD), :]
    queries = q_ref[tile, pair]
    peaks = ml_ref[tile, pair, 0]
    totals = ml_ref[tile, pair, 1]
    lanes = [slice(head * LEN, (head + 1) * LEN) for head in range(GROUP)]
    scores = [
        jnp.dot(k_tile, queries[:, at], preferred_element_type=jnp.float32) for at in lanes
    ]
    if bounds is not None:
        scores = [jnp.where(bounds, s, MASKED) for s in scores]
    new = [
        jnp.maximum(peaks[:, at], jnp.max(s, axis=0, keepdims=True)) for at, s in zip(lanes, scores)
    ]
    weights = [jnp.exp2((s - peak) * COEF) for s, peak in zip(scores, new)]
    products = [
        jnp.dot(v_turned, w.astype(jnp.bfloat16), preferred_element_type=jnp.float32) for w in weights
    ]
    fades = [jnp.exp2((peaks[:, at] - peak) * COEF) for at, peak in zip(lanes, new)]
    sums = [jnp.sum(w, axis=0, keepdims=True) for w in weights]
    for head, at in enumerate(lanes):
        ml_ref[tile, pair, 0, :, at] = new[head]
        ml_ref[tile, pair, 1, :, at] = totals[:, at] * fades[head] + sums[head]
        acc_ref[tile, pair, :, at] = acc_ref[tile, pair, :, at] * fades[head] + products[head]


def attend_kernel(sources, later, n_infos, first, finish, final, *refs):
    refs = list(refs)
    take = lambda n: [refs.pop(0) for _ in range(n)]
    count = len(sources)
    info_in = take(n_infos)
    q_in = take(2)
    chunk_in = take(count)
    state_in = [] if first else take(3)
    if final:
        take(2)
    results = take(2) if finish else []
    state_out = [] if final else take(3)
    q_ref, chunk_ref, info_ref = take(3)
    state = acc_ref, ml_ref, best_ref = take(3)
    buffers = take(2) if finish else []
    info_sem, q_sem, chunk_sem, state_sem = take(4)
    stretch = lax.axis_index("ctx")
    pairs = acc_ref.shape[1]

    copy_of = pltpu.make_async_copy
    info_copies = [
        copy_of(ref.at[INFO:, :], info_ref.at[i], info_sem.at[i]) for i, ref in enumerate(info_in)
    ]
    state_copies = [
        copy_of(source, target, state_sem.at[i]) for i, (source, target) in enumerate(zip(state_in, state))
    ]
    bulk = [copy_of(q_in[i], q_ref.at[i], q_sem.at[i]) for i in range(2)]
    bulk += [copy_of(chunk_in[i], chunk_ref.at[i], chunk_sem.at[i]) for i in range(count)]
    bulk += state_copies[:2]
    for copy in info_copies + state_copies[2:]:
        copy.start()
    if not final:
        for copy in bulk:
            copy.start()
    if first:
        acc_ref[...] = jnp.zeros_like(acc_ref)
        ml_ref[:, :, 0] = jnp.full_like(ml_ref[:, :, 0], MASKED)
        ml_ref[:, :, 1] = jnp.zeros_like(ml_ref[:, :, 1])
        best_ref[...] = jnp.full_like(best_ref, -1.0)

    for copy in info_copies + state_copies[2:]:
        copy.wait()
    low, high = [], []
    for tile in range(2):
        for block, found in ((0, low), (1, high)):
            row = 2 * tile + block
            number = (2 * (stretch ^ tile) + block).astype(jnp.float32)
            best = best_ref[row]
            for i in range(n_infos):
                entries = info_ref[i, 0:1, :HD].astype(jnp.float32)
                best = jnp.maximum(best, jnp.where(entries <= number, entries, -1.0))
            best_ref[row] = best
            found.append(jnp.max(best).astype(jnp.int32))

    second = lax.rem(lax.div(stretch, 2), 2) == 1

    def origins(table):
        return [(stretch ^ bits) - jnp.where(second, upper, lower) for bits, lower, upper in table]

    source_of = origins(sources)

    def view(source, tile, low_start, high_start):
        where = stretch ^ tile
        first_key, first_query = source * LEN, where * LEN
        low_limit = jnp.maximum(low_start * BLK, first_query - WINDOW + 1)
        seen = (source >= 0) & (source <= where) & (first_key + LEN > low_limit)
        high_limit = jnp.maximum(high_start * BLK, first_query + LEN - WINDOW)
        whole = (source < where) & (first_key >= high_limit)
        return seen, whole

    def any_seen(table):
        return functools.reduce(
            jnp.logical_or,
            [view(source, tile, low[tile], high[tile])[0] for source in table for tile in range(2)],
        )

    busy = any_seen(source_of)

    def visit(step, _):
        chunk, tile = lax.div(step, 2), lax.rem(step, 2)
        source = source_of[0]
        for i in range(1, count):
            source = jnp.where(chunk == i, source_of[i], source)
        low_start = jnp.where(tile == 0, low[0], low[1])
        high_start = jnp.where(tile == 0, high[0], high[1])
        seen, whole = view(source, tile, low_start, high_start)

        def all_heads(masked):
            bounds = None
            if masked:
                lane = lax.broadcasted_iota(jnp.int32, (1, LEN), 1)
                query_pos = (stretch ^ tile) * LEN + lane
                start = jnp.where(lane < BLK, low_start, high_start) * BLK
                least = jnp.maximum(start, query_pos - (WINDOW - 1))
                key_pos = source * LEN + lax.broadcasted_iota(jnp.int32, (LEN, LEN), 0)
                bounds = (key_pos <= query_pos) & (key_pos >= least)

            def one_pair(pair, _):
                pair_step(q_ref, chunk_ref, acc_ref, ml_ref, chunk, tile, pair, bounds)
                return 0

            lax.fori_loop(0, pairs, one_pair, 0)

        @pl.when(seen & whole)
        def _():
            all_heads(False)

        @pl.when(seen & jnp.logical_not(whole))
        def _():
            all_heads(True)

        return 0

    def finished():
        sinks = (results[0].at[:, columns(my_half(False), results[1].shape[1])], results[1])
        leaving = []
        for tile in (1, 0):
            lane = lax.broadcasted_iota(jnp.int32, (1, WIDE), 1)
            start = jnp.where(lax.rem(lane, LEN) < BLK, low[tile], high[tile])
            active = (start >= 0) | ((stretch ^ tile) >= 1)
            for pair in range(pairs):
                scale = jnp.where(active, 1.0 / ml_ref[tile, pair, 1], 0.0)
                for head in range(GROUP):
                    lanes = slice(head * LEN, (head + 1) * LEN)
                    blended = (acc_ref[tile, pair, :, lanes] * scale[:, lanes]).astype(jnp.bfloat16)
                    at = (pair * GROUP + head) * HD
                    buffers[tile][:, at : at + HD] = blended.T
            copy = copy_of(buffers[tile], sinks[tile], q_sem.at[tile])
            copy.start()
            leaving.append(copy)
        for copy in leaving:
            copy.wait()

    if final:

        @pl.when(busy)
        def _():
            for copy in bulk:
                copy.start()
            for copy in bulk:
                copy.wait()
            lax.fori_loop(0, 2 * count, visit, 0)
            finished()

        return

    for copy in bulk:
        copy.wait()

    @pl.when(busy)
    def _():
        lax.fori_loop(0, 2 * count, visit, 0)

    back = [
        copy_of(source, target, state_sem.at[i]) for i, (source, target) in enumerate(zip(state, state_out))
    ]
    back[2].start()
    back[2].wait()
    goes_on = any_seen(origins(later)) if finish else True

    @pl.when((busy | first) & goes_on)
    def _():
        for copy in back[:2]:
            copy.start()
        for copy in back[:2]:
            copy.wait()

    if finish:
        pl.when(jnp.logical_not(goes_on))(finished)


def attend(infos, qs, chunks, sources, state, later=None, results=None, width=0):
    finish, final, first = width > 0, results is not None, state is None
    pairs = qs[0].shape[0]
    args = list(infos) + list(qs) + list(chunks)
    state_shapes = (2, pairs, HD, WIDE), (2, pairs, 2, 1, WIDE), (4, 1, HD)
    half = pairs * GROUP * HD
    shapes = [jax.ShapeDtypeStruct((LEN, w), jnp.bfloat16) for w in (width, half)] if finish else []
    aliases = {}
    if not first:
        if not final:
            aliases = {len(args) + i: len(shapes) + i for i in range(3)}
        args += list(state)
    if final:
        aliases = {len(args) + i: i for i in range(2)}
        args += list(results)
    else:
        shapes += [jax.ShapeDtypeStruct(s, jnp.float32) for s in state_shapes]
    scratch = [
        pltpu.VMEM((2,) + qs[0].shape, jnp.bfloat16),
        pltpu.VMEM((len(chunks),) + CHUNK, jnp.bfloat16),
        pltpu.VMEM((max(len(infos), 1), 16, LEN), jnp.bfloat16),
    ] + [pltpu.VMEM(s, jnp.float32) for s in state_shapes]
    if finish:
        scratch += [pltpu.VMEM((LEN, half), jnp.bfloat16)] * 2
    scratch += [pltpu.SemaphoreType.DMA((n,)) for n in (max(len(infos), 1), 2, len(chunks), 3)]
    elements = len(chunks) * 2 * pairs * LEN * WIDE
    return pl.pallas_call(
        functools.partial(attend_kernel, sources, later, len(infos), first, finish, final),
        out_shape=shapes,
        in_specs=[ANY] * len(args),
        out_specs=[ANY] * len(shapes),
        scratch_shapes=scratch,
        input_output_aliases=aliases,
        cost_estimate=pl.CostEstimate(
            flops=4 * HD * elements, bytes_accessed=6 << 20, transcendentals=elements
        ),
        compiler_params=pltpu.CompilerParams(vmem_limit_bytes=LIMIT),
        name="attend",
    )(*args)


def steps(queries, keys, values, doc_starts):
    rows, width = queries.shape
    assert rows == LEN and keys.shape[1] == 4 * HD and lax.axis_size("ctx") % 4 == 0
    own = prep_kv(keys, values, (doc_starts,), False)
    a_own = shifted(own, 4)
    across = exchanged(doc_starts, 2)
    q_send = prep_q(queries, True)
    q_pair = exchanged(q_send, 1)
    send = prep_kv(keys, values, (doc_starts, across), True)
    pair = exchanged(send, 1)
    qs = (prep_q(queries, False), q_pair)
    a_pair = shifted(pair, 4)
    x_own = crossed(own, a_own)
    b_own = shifted(a_own, 4)
    state = attend((own, pair), qs, (own,), ((0, 0, 0),), None)
    x_pair = crossed(pair, a_pair)
    b_pair = shifted(a_pair, 4)
    state = attend(
        (a_own, a_pair, x_own), qs, (pair, a_own), ((1, 0, 0), (0, 4, 4)), state
    )
    xb_own = crossed(a_own, b_own)
    state = attend((), qs, (a_pair, x_own), ((1, 4, 4), (2, 4, 0)), state)
    xb_pair = crossed(a_pair, b_pair)
    state = attend((), qs, (x_pair,), ((3, 4, 0),), state)
    rest = ((3, 8, 4),)
    full, out_send, *state = attend(
        (b_own, b_pair, xb_own),
        qs,
        (b_own, b_pair, xb_own),
        ((0, 8, 8), (1, 8, 8), (2, 8, 4)),
        state,
        later=rest,
        width=width,
    )
    full, out_send = attend((), qs, (xb_pair,), rest, state, results=(full, out_send), width=width)
    return merge(exchanged(out_send, 1), full)


def solution(mesh):
    spec = P(("groups", "ctx"), None)
    return jax.shard_map(steps, mesh=mesh, in_specs=(spec,) * 4, out_specs=spec, check_vma=False)
```

```python
import functools
import math

import jax
import jax.numpy as jnp
from jax import lax
from jax.experimental import pallas as pl
from jax.experimental.pallas import tpu as pltpu
from jax.sharding import PartitionSpec as P

HD = 128
WINDOW = 2048
BLK = 128
LEN = 256
GROUP = 4
WIDE = GROUP * LEN
INFO = 2 * LEN
CHUNK = (INFO + 16, LEN)
MASKED = -1e30
COEF = math.log2(math.e) / math.sqrt(HD)

VMEM = pl.BlockSpec(memory_space=pltpu.VMEM)
SMEM = pl.BlockSpec(memory_space=pltpu.SMEM)
ANY = pl.BlockSpec(memory_space=pl.ANY)
LIMIT = 20 << 20
SMALL = pltpu.CompilerParams(vmem_limit_bytes=4 << 20)
BOTH = (0, 1)


def exchanged(x, bit):
    n = lax.axis_size("ctx")
    return lax.ppermute(x, "ctx", [(i, i ^ bit) for i in range(n)])


def shifted(x, distance):
    n = lax.axis_size("ctx")
    return lax.ppermute(x, "ctx", [(i, (i + distance) % n) for i in range(n)])


def in_hbm(x):
    return pltpu.with_memory_space_constraint(x, pltpu.HBM)


def my_half(other):
    core = lax.rem(lax.axis_index("ctx"), 2)
    return 1 - core if other else core


def columns(index, width):
    return pl.ds(pl.multiple_of(index * width, width), width)


def prep_kv_kernel(other, count, k_ref, v_ref, *refs):
    table_refs, (out_ref, k_buf, v_buf, turned, info_buf) = refs[:count], refs[count : count + 5]
    tables, sems, out_sems = refs[count + 5 :]
    pick = my_half(other)
    rows = LEN // 2
    fetch = pltpu.make_async_copy
    starts = [fetch(ref, tables.at[i], sems.at[4 + i]) for i, ref in enumerate(table_refs)]
    v_in = [
        fetch(v_ref.at[i * rows : (i + 1) * rows, columns(pick, 2 * HD)], v_buf.at[i], sems.at[i])
        for i in range(2)
    ]
    k_in = [
        fetch(k_ref.at[i * rows : (i + 1) * rows, columns(pick, 2 * HD)], k_buf.at[i], sems.at[2 + i])
        for i in range(2)
    ]
    for copy in starts + v_in + k_in:
        copy.start()
    leaving = []

    def leave(source, first, last):
        copy = fetch(source, out_ref.at[first:last], out_sems.at[len(leaving)])
        copy.start()
        leaving.append(copy)

    for copy in starts:
        copy.wait()
    lane = lax.broadcasted_iota(jnp.int32, (16, LEN), 1)
    info = jnp.full((16, LEN), -1, jnp.int32)
    for i in range(count):
        for col in range(2):
            info = jnp.where(lane == 2 * i + col, tables[i, 0, col], info)
    info_buf[...] = info.astype(jnp.float32).astype(jnp.bfloat16)
    leave(info_buf, INFO, INFO + 16)
    for i, copy in enumerate(v_in):
        copy.wait()
        for pair in range(2):
            turned[pair * HD : (pair + 1) * HD, i * rows : (i + 1) * rows] = v_buf[
                i, :, pair * HD : (pair + 1) * HD
            ].T
    leave(turned, LEN, INFO)
    for i, copy in enumerate(k_in):
        copy.wait()
        leave(k_buf.at[i], i * rows, (i + 1) * rows)
    for copy in leaving:
        copy.wait()


def prep_kv(keys, values, tables, other):
    return pl.pallas_call(
        functools.partial(prep_kv_kernel, other, len(tables)),
        out_shape=jax.ShapeDtypeStruct(CHUNK, jnp.bfloat16),
        in_specs=[ANY] * (2 + len(tables)),
        out_specs=ANY,
        scratch_shapes=[
            pltpu.VMEM((2, LEN // 2, LEN), jnp.bfloat16),
            pltpu.VMEM((2, LEN // 2, LEN), jnp.bfloat16),
            pltpu.VMEM((LEN, LEN), jnp.bfloat16),
            pltpu.VMEM((16, LEN), jnp.bfloat16),
            pltpu.SMEM((len(tables), 1, 2), jnp.int32),
            pltpu.SemaphoreType.DMA((4 + len(tables),)),
            pltpu.SemaphoreType.DMA((4,)),
        ],
        compiler_params=SMALL,
        name="prep_kv",
    )(in_hbm(keys), in_hbm(values), *tables)


def prep_q_kernel(other, q_ref, out_ref, q_buf, sems):
    pick = my_half(other)
    pairs = out_ref.shape[0]
    copies = [
        pltpu.make_async_copy(
            q_ref.at[:, columns(pick * pairs + pair, GROUP * HD)], q_buf.at[pair], sems.at[pair]
        )
        for pair in range(pairs)
    ]
    for copy in copies:
        copy.start()
    for pair, copy in enumerate(copies):
        copy.wait()
        for head in range(GROUP):
            out_ref[pair, :, head * LEN : (head + 1) * LEN] = q_buf[
                pair, :, head * HD : (head + 1) * HD
            ].T


def prep_q(queries, other):
    pairs = queries.shape[1] // (2 * GROUP * HD)
    return pl.pallas_call(
        functools.partial(prep_q_kernel, other),
        out_shape=jax.ShapeDtypeStruct((pairs, HD, WIDE), jnp.bfloat16),
        in_specs=[ANY],
        out_specs=VMEM,
        scratch_shapes=[
            pltpu.VMEM((pairs, LEN, GROUP * HD), jnp.bfloat16),
            pltpu.SemaphoreType.DMA((pairs,)),
        ],
        compiler_params=SMALL,
        name="prep_q",
    )(in_hbm(queries))


def pick_kernel(lower_ref, upper_ref, out_ref, sem):
    second = lax.rem(lax.div(lax.axis_index("ctx"), 2), 2) == 1

    @pl.when(second)
    def _():
        pltpu.make_async_copy(upper_ref, out_ref, sem).start()

    @pl.when(jnp.logical_not(second))
    def _():
        pltpu.make_async_copy(lower_ref, out_ref, sem).start()

    pltpu.make_async_copy(lower_ref, out_ref, sem).wait()


def crossed(lower, upper):
    picked = pl.pallas_call(
        pick_kernel,
        out_shape=jax.ShapeDtypeStruct(lower.shape, lower.dtype),
        in_specs=[ANY] * 2,
        out_specs=VMEM,
        scratch_shapes=[pltpu.SemaphoreType.DMA],
        compiler_params=pltpu.CompilerParams(vmem_limit_bytes=2 << 20),
        name="pick",
    )(lower, upper)
    return exchanged(picked, 2)


def merge_kernel(got_ref, full_in, full_ref, sem):
    copy = pltpu.make_async_copy(got_ref, full_ref.at[:, columns(my_half(True), got_ref.shape[1])], sem)
    copy.start()
    copy.wait()


def merge(got, full):
    return pl.pallas_call(
        merge_kernel,
        out_shape=jax.ShapeDtypeStruct(full.shape, full.dtype),
        in_specs=[VMEM, ANY],
        out_specs=ANY,
        scratch_shapes=[pltpu.SemaphoreType.DMA],
        input_output_aliases={1: 0},
        compiler_params=SMALL,
        name="merge",
    )(got, full)


def pair_step(q_ref, chunk_ref, acc_ref, ml_ref, chunk, tile, pair, bounds):
    k_tile = chunk_ref[chunk, :LEN, pl.ds(pl.multiple_of(pair * HD, HD), HD)]
    v_turned = chunk_ref[chunk, pl.ds(pl.multiple_of(LEN + pair * HD, HD), HD), :]
    queries = q_ref[tile, pair]
    peaks = ml_ref[tile, pair, 0]
    totals = ml_ref[tile, pair, 1]
    lanes = [slice(head * LEN, (head + 1) * LEN) for head in range(GROUP)]
    scores = [
        jnp.dot(k_tile, queries[:, at], preferred_element_type=jnp.float32) for at in lanes
    ]
    if bounds is not None:
        scores = [jnp.where(bounds, s, MASKED) for s in scores]
    new = [
        jnp.maximum(peaks[:, at], jnp.max(s, axis=0, keepdims=True)) for at, s in zip(lanes, scores)
    ]
    weights = [jnp.exp2((s - peak) * COEF) for s, peak in zip(scores, new)]
    products = [
        jnp.dot(v_turned, w.astype(jnp.bfloat16), preferred_element_type=jnp.float32) for w in weights
    ]
    fades = [jnp.exp2((peaks[:, at] - peak) * COEF) for at, peak in zip(lanes, new)]
    sums = [jnp.sum(w, axis=0, keepdims=True) for w in weights]
    for head, at in enumerate(lanes):
        ml_ref[tile, pair, 0, :, at] = new[head]
        ml_ref[tile, pair, 1, :, at] = totals[:, at] * fades[head] + sums[head]
        acc_ref[tile, pair, :, at] = acc_ref[tile, pair, :, at] * fades[head] + products[head]


def attend_kernel(sources, later, n_infos, first, finish, final, *refs):
    refs = list(refs)
    take = lambda n: [refs.pop(0) for _ in range(n)]
    count = len(sources)
    info_in = take(n_infos)
    q_in = take(2)
    chunk_in = take(count)
    state_in = [] if first else take(3)
    if final:
        take(2)
    results = take(2) if finish else []
    state_out = [] if final else take(3)
    q_ref, chunk_ref, info_ref = take(3)
    state = acc_ref, ml_ref, best_ref = take(3)
    buffers = take(2) if finish else []
    info_sem, q_sem, chunk_sem, state_sem = take(4)
    stretch = lax.axis_index("ctx")
    pairs = acc_ref.shape[1]

    copy_of = pltpu.make_async_copy
    info_copies = [
        copy_of(ref.at[INFO:, :], info_ref.at[i], info_sem.at[i]) for i, ref in enumerate(info_in)
    ]
    state_copies = [
        copy_of(source, target, state_sem.at[i]) for i, (source, target) in enumerate(zip(state_in, state))
    ]
    bulk = [copy_of(q_in[i], q_ref.at[i], q_sem.at[i]) for i in range(2)]
    bulk += [copy_of(chunk_in[i], chunk_ref.at[i], chunk_sem.at[i]) for i in range(count)]
    bulk += state_copies[:2]
    for copy in info_copies + state_copies[2:]:
        copy.start()
    if not final:
        for copy in bulk:
            copy.start()
    if first:
        acc_ref[...] = jnp.zeros_like(acc_ref)
        ml_ref[:, :, 0] = jnp.full_like(ml_ref[:, :, 0], MASKED)
        ml_ref[:, :, 1] = jnp.zeros_like(ml_ref[:, :, 1])
        best_ref[...] = jnp.full_like(best_ref, -1.0)

    for copy in info_copies + state_copies[2:]:
        copy.wait()
    low, high = [], []
    for tile in range(2):
        for block, found in ((0, low), (1, high)):
            row = 2 * tile + block
            number = (2 * (stretch ^ tile) + block).astype(jnp.float32)
            best = best_ref[row]
            for i in range(n_infos):
                entries = info_ref[i, 0:1, :HD].astype(jnp.float32)
                best = jnp.maximum(best, jnp.where(entries <= number, entries, -1.0))
            best_ref[row] = best
            found.append(jnp.max(best).astype(jnp.int32))

    second = lax.rem(lax.div(stretch, 2), 2) == 1

    def origins(table):
        return [(stretch ^ bits) - jnp.where(second, upper, lower) for bits, lower, upper, *_ in table]

    source_of = origins(sources)

    def view(source, tile, low_start, high_start):
        where = stretch ^ tile
        first_key, first_query = source * LEN, where * LEN
        low_limit = jnp.maximum(low_start * BLK, first_query - WINDOW + 1)
        seen = (source >= 0) & (source <= where) & (first_key + LEN > low_limit)
        high_limit = jnp.maximum(high_start * BLK, first_query + LEN - WINDOW)
        whole = (source < where) & (first_key >= high_limit)
        return seen, whole

    def any_seen(table):
        return functools.reduce(
            jnp.logical_or,
            [view(source, tile, low[tile], high[tile])[0] for source in table for tile in range(2)],
        )

    busy = any_seen(source_of)

    def visit(step, _):
        chunk, tile = lax.div(step, 2), lax.rem(step, 2)
        source = source_of[0]
        for i in range(1, count):
            source = jnp.where(chunk == i, source_of[i], source)
        low_start = jnp.where(tile == 0, low[0], low[1])
        high_start = jnp.where(tile == 0, high[0], high[1])
        seen, whole = view(source, tile, low_start, high_start)
        for i, (*_, tiles) in enumerate(sources):
            for left_out in set(range(2)) - set(tiles):
                seen &= jnp.logical_not((chunk == i) & (tile == left_out))

        def all_heads(masked):
            bounds = None
            if masked:
                lane = lax.broadcasted_iota(jnp.int32, (1, LEN), 1)
                query_pos = (stretch ^ tile) * LEN + lane
                start = jnp.where(lane < BLK, low_start, high_start) * BLK
                least = jnp.maximum(start, query_pos - (WINDOW - 1))
                key_pos = source * LEN + lax.broadcasted_iota(jnp.int32, (LEN, LEN), 0)
                bounds = (key_pos <= query_pos) & (key_pos >= least)

            def one_pair(pair, _):
                pair_step(q_ref, chunk_ref, acc_ref, ml_ref, chunk, tile, pair, bounds)
                return 0

            lax.fori_loop(0, pairs, one_pair, 0)

        @pl.when(seen & whole)
        def _():
            all_heads(False)

        @pl.when(seen & jnp.logical_not(whole))
        def _():
            all_heads(True)

        return 0

    def finished():
        sinks = (results[0].at[:, columns(my_half(False), results[1].shape[1])], results[1])
        leaving = []
        for tile in (1, 0):
            lane = lax.broadcasted_iota(jnp.int32, (1, WIDE), 1)
            start = jnp.where(lax.rem(lane, LEN) < BLK, low[tile], high[tile])
            active = (start >= 0) | ((stretch ^ tile) >= 1)
            for pair in range(pairs):
                scale = jnp.where(active, 1.0 / ml_ref[tile, pair, 1], 0.0)
                for head in range(GROUP):
                    lanes = slice(head * LEN, (head + 1) * LEN)
                    blended = (acc_ref[tile, pair, :, lanes] * scale[:, lanes]).astype(jnp.bfloat16)
                    at = (pair * GROUP + head) * HD
                    buffers[tile][:, at : at + HD] = blended.T
            copy = copy_of(buffers[tile], sinks[tile], q_sem.at[tile])
            copy.start()
            leaving.append(copy)
        for copy in leaving:
            copy.wait()

    if final:

        @pl.when(busy)
        def _():
            for copy in bulk:
                copy.start()
            for copy in bulk:
                copy.wait()
            lax.fori_loop(0, 2 * count, visit, 0)
            finished()

        return

    for copy in bulk:
        copy.wait()

    @pl.when(busy)
    def _():
        lax.fori_loop(0, 2 * count, visit, 0)

    back = [
        copy_of(source, target, state_sem.at[i]) for i, (source, target) in enumerate(zip(state, state_out))
    ]
    back[2].start()
    back[2].wait()
    goes_on = any_seen(origins(later)) if finish else True

    @pl.when((busy | first) & goes_on)
    def _():
        for copy in back[:2]:
            copy.start()
        for copy in back[:2]:
            copy.wait()

    if finish:
        pl.when(jnp.logical_not(goes_on))(finished)


def attend(infos, qs, chunks, sources, state, later=None, results=None, width=0):
    finish, final, first = width > 0, results is not None, state is None
    pairs = qs[0].shape[0]
    args = list(infos) + list(qs) + list(chunks)
    state_shapes = (2, pairs, HD, WIDE), (2, pairs, 2, 1, WIDE), (4, 1, HD)
    half = pairs * GROUP * HD
    shapes = [jax.ShapeDtypeStruct((LEN, w), jnp.bfloat16) for w in (width, half)] if finish else []
    aliases = {}
    if not first:
        if not final:
            aliases = {len(args) + i: len(shapes) + i for i in range(3)}
        args += list(state)
    if final:
        aliases = {len(args) + i: i for i in range(2)}
        args += list(results)
    else:
        shapes += [jax.ShapeDtypeStruct(s, jnp.float32) for s in state_shapes]
    scratch = [
        pltpu.VMEM((2,) + qs[0].shape, jnp.bfloat16),
        pltpu.VMEM((len(chunks),) + CHUNK, jnp.bfloat16),
        pltpu.VMEM((max(len(infos), 1), 16, LEN), jnp.bfloat16),
    ] + [pltpu.VMEM(s, jnp.float32) for s in state_shapes]
    if finish:
        scratch += [pltpu.VMEM((LEN, half), jnp.bfloat16)] * 2
    scratch += [pltpu.SemaphoreType.DMA((n,)) for n in (max(len(infos), 1), 2, len(chunks), 3)]
    elements = len(chunks) * 2 * pairs * LEN * WIDE
    return pl.pallas_call(
        functools.partial(attend_kernel, sources, later, len(infos), first, finish, final),
        out_shape=shapes,
        in_specs=[ANY] * len(args),
        out_specs=[ANY] * len(shapes),
        scratch_shapes=scratch,
        input_output_aliases=aliases,
        cost_estimate=pl.CostEstimate(
            flops=4 * HD * elements, bytes_accessed=6 << 20, transcendentals=elements
        ),
        compiler_params=pltpu.CompilerParams(vmem_limit_bytes=LIMIT),
        name="attend",
    )(*args)


def steps(queries, keys, values, doc_starts):
    rows, width = queries.shape
    assert rows == LEN and keys.shape[1] == 4 * HD and lax.axis_size("ctx") % 4 == 0
    own = prep_kv(keys, values, (in_hbm(doc_starts),), False)
    a_own = shifted(own, 4)
    across = exchanged(doc_starts, 2)
    q_send = prep_q(queries, True)
    q_pair = exchanged(q_send, 1)
    send = prep_kv(keys, values, (in_hbm(doc_starts), across), True)
    pair = exchanged(send, 1)
    qs = (prep_q(queries, False), q_pair)
    a_pair = shifted(pair, 4)
    x_own = crossed(own, a_own)
    b_own = shifted(a_own, 4)
    state = attend(
        (own, pair), qs, (own, pair), ((0, 0, 0, BOTH), (1, 0, 0, (0,))), None
    )
    x_pair = crossed(pair, a_pair)
    b_pair = shifted(a_pair, 4)
    state = attend(
        (a_own, a_pair, x_own), qs, (pair, a_own), ((1, 0, 0, (1,)), (0, 4, 4, BOTH)), state
    )
    xb_own = crossed(a_own, b_own)
    state = attend((), qs, (a_pair, x_own), ((1, 4, 4, BOTH), (2, 4, 0, BOTH)), state)
    xb_pair = crossed(a_pair, b_pair)
    state = attend((), qs, (x_pair,), ((3, 4, 0, BOTH),), state)
    rest = ((3, 8, 4, BOTH),)
    full, out_send, *state = attend(
        (b_own, b_pair, xb_own),
        qs,
        (b_own, b_pair, xb_own),
        ((0, 8, 8, BOTH), (1, 8, 8, BOTH), (2, 8, 4, BOTH)),
        state,
        later=rest,
        width=width,
    )
    full, out_send = attend((), qs, (xb_pair,), rest, state, results=(full, out_send), width=width)
    return merge(exchanged(out_send, 1), full)


def solution(mesh):
    spec = P(("groups", "ctx"), None)
    return jax.shard_map(steps, mesh=mesh, in_specs=(spec,) * 4, out_specs=spec, check_vma=False)
```
